128 devices in a mesh: dp: 16 (over z, x_lo, core), expert: 8 (over x_hi, y).
Axes of the slice: x: 4 (x_hi: 2, x_lo: 2; x = x_hi * 2 + x_lo), y: 4, z: 4, core: 2. Of those that a mesh axis runs over, the one named last changes fastest.
Arguments:
- features: bfloat16 [2048, 1024], P('dp'), may hold values from -6 to 6
- cross_weight: bfloat16 [1, 1024, 1024], replicated, may hold values from -0.1875 to 0.1875
- cross_bias: float32 [1, 1024], replicated, may hold values from -3 to 3
- gate_weight: bfloat16 [1024, 64], replicated, may hold values from -0.1875 to 0.1875
- gate_offset: float32 [64], replicated, may hold values from -3 to 3
- up_weight: bfloat16 [16, 1024, 8192], P('expert', None, 'dp'), may hold values from -0.1875 to 0.1875
- down_weight: bfloat16 [16, 8192, 1024], P('expert', 'dp'), may hold values from -0.0625 to 0.0625
- task_grad: bfloat16 [2048, 4, 1024], P('dp'), may hold values from -6 to 6
Outputs:
- task_mixed: bfloat16 [2048, 4, 1024], P('dp')
- feature_grad: bfloat16 [2048, 1024], P('dp')
- up_grad: bfloat16 [16, 1024, 8192], P('expert', None, 'dp')
- down_grad: bfloat16 [16, 8192, 1024], P('expert', 'dp')
- cross_grad: float32 [1, 1024, 1024], replicated
- bias_grad: float32 [1, 1024], replicated
- gating_grad: float32 [1024, 64], replicated
- offset_grad: float32 [64], replicated
The draws below stay inside these ranges and needn't reach their ends.
All inputs are finite; a program needn't handle non-finite values.
Results may differ from the reference program's by a relative error of at most 0.012.
Values may be sent and summed in bfloat16 or wider, within the bound.
A program may use at most 192 MiB of HBM per device.

```python
import jax
import jax.numpy as jnp
from jax import lax

D = 1024
HIDDEN_SIZE = 8192
EXPERTS = 16
TASKS = 4
LAYERS = 1
ROWS = 2048


def block_scale(stream_key, dims, shards, least, high):
    def one(dim, blocks):
        steps = jax.random.uniform(jax.random.fold_in(jax.random.fold_in(stream_key, 6), dim), (blocks,), jnp.float32, least / len(shards), high / len(shards))
        return jnp.repeat(jnp.exp(steps), dims[dim] // blocks).reshape((-1,) + (1,) * (len(dims) - dim - 1))

    level = one(*shards[0])
    for cut in shards[1:]:
        level = level * one(*cut)
    return level


def normal_values(stream_key, shape, spread, bound, split=(), kind=jnp.bfloat16):
    array = spread * jax.random.normal(stream_key, shape, jnp.float32)
    if split:
        array = array * block_scale(stream_key, shape, split, -0.22, 0.18)
    return jnp.clip(array, -bound, bound).astype(kind)


def setup_inputs(seed: int = 0) -> dict:
    key_list = jax.random.split(jax.random.key(seed), 9)
    return {
        "features": normal_values(key_list[0], (ROWS, D), 1.0, 6.0, ((0, 16),)),
        "cross_weight": normal_values(key_list[1], (LAYERS, D, D), D ** -0.5, 0.1875),
        "cross_bias": normal_values(key_list[2], (LAYERS, D), 0.5, 3.0, (), jnp.float32),
        "gate_weight": normal_values(key_list[3], (D, TASKS * EXPERTS), D ** -0.5, 0.1875),
        "gate_offset": normal_values(key_list[4], (TASKS * EXPERTS,), 1.0, 3.0, (), jnp.float32),
        "up_weight": normal_values(key_list[5], (EXPERTS, D, HIDDEN_SIZE), D ** -0.5, 0.1875, ((0, 8), (2, 16))),
        "down_weight": normal_values(key_list[6], (EXPERTS, HIDDEN_SIZE, D), HIDDEN_SIZE ** -0.5, 0.0625, ((0, 8), (1, 16))),
        "task_grad": normal_values(key_list[7], (ROWS, TASKS, D), 1.0, 6.0, ((0, 16),)),
    }


def cross_forward(features, cross_weight, cross_bias):
    states = features.astype(jnp.float32)
    rounded = []
    updates = []
    for layer in range(cross_weight.shape[0]):
        low = states.astype(jnp.bfloat16)
        update = jnp.dot(low, cross_weight[layer], preferred_element_type=jnp.float32) + cross_bias[layer]
        states = features.astype(jnp.float32) * update + states
        rounded.append(low)
        updates.append(update)
    return states, rounded, updates


def cross_backward(features, cross_weight, rounded, updates, upstream):
    base = features.astype(jnp.float32)
    direct = jnp.zeros_like(upstream)
    weight_terms = []
    bias_terms = []
    for layer in reversed(range(len(rounded))):
        scaled = (upstream * base).astype(jnp.bfloat16)
        weight_terms.insert(0, jnp.dot(rounded[layer].T, scaled, preferred_element_type=jnp.float32))
        bias_terms.insert(0, jnp.sum(scaled.astype(jnp.float32), axis=0))
        direct = direct + upstream * updates[layer]
        upstream = upstream + jnp.dot(scaled, cross_weight[layer].T, preferred_element_type=jnp.float32)
    return (upstream + direct).astype(jnp.bfloat16), jnp.stack(weight_terms), jnp.stack(bias_terms)


def gating(shared, gate_weight, gate_offset):
    logits = jnp.dot(shared, gate_weight, preferred_element_type=jnp.float32) + gate_offset
    logits = logits.reshape(shared.shape[0], TASKS, EXPERTS)
    expo = jnp.exp(logits)
    return expo / jnp.sum(expo, axis=-1, keepdims=True)


def reference(features, cross_weight, cross_bias, gate_weight, gate_offset, up_weight, down_weight, task_grad):
    states, rounded, updates = cross_forward(features, cross_weight, cross_bias)
    shared = states.astype(jnp.bfloat16)
    gate_probs = gating(shared, gate_weight, gate_offset)
    row_count = shared.shape[0]

    def expert_forward(carry, weights):
        hidden_pre = jnp.dot(shared, weights[0], preferred_element_type=jnp.float32)
        hidden_act = (hidden_pre * jax.nn.sigmoid(hidden_pre)).astype(jnp.bfloat16)
        summed = jnp.dot(hidden_act, weights[1], preferred_element_type=jnp.float32)
        return carry, summed

    unused, expert_out = lax.scan(expert_forward, jnp.float32(0.0), (up_weight, down_weight))
    high = lax.Precision.HIGHEST
    task_mixed = jnp.einsum('rte,erd->rtd', gate_probs, expert_out, precision=high).astype(jnp.bfloat16)
    grad_wide = task_grad.astype(jnp.float32)
    out_grad = jnp.einsum('rte,rtd->erd', gate_probs, grad_wide, precision=high).astype(jnp.bfloat16)
    gate_grad = jnp.einsum('rtd,erd->rte', grad_wide, expert_out, precision=high)
    logit_grad = gate_probs * (gate_grad - jnp.sum(gate_probs * gate_grad, axis=-1, keepdims=True))
    logit_low = logit_grad.reshape(row_count, TASKS * EXPERTS).astype(jnp.bfloat16)

    def expert_backward(carry, weights):
        first, second, grad_out = weights
        hidden_pre = jnp.dot(shared, first, preferred_element_type=jnp.float32)
        sig = jax.nn.sigmoid(hidden_pre)
        hidden_act = (hidden_pre * sig).astype(jnp.bfloat16)
        hidden_grad = jnp.dot(grad_out, second.T, preferred_element_type=jnp.float32)
        pre_grad = (hidden_grad * sig * (1.0 + hidden_pre * (1.0 - sig))).astype(jnp.bfloat16)
        second_grad = jnp.dot(hidden_act.T, grad_out, preferred_element_type=jnp.float32).astype(jnp.bfloat16)
        first_grad = jnp.dot(shared.T, pre_grad, preferred_element_type=jnp.float32).astype(jnp.bfloat16)
        carry = carry + jnp.dot(pre_grad, first.T, preferred_element_type=jnp.float32)
        return carry, (first_grad, second_grad)

    start_grad = jnp.zeros(shared.shape, jnp.float32)
    shared_grad, grads = lax.scan(expert_backward, start_grad, (up_weight, down_weight, out_grad))
    shared_grad = shared_grad + jnp.dot(logit_low, gate_weight.T, preferred_element_type=jnp.float32)
    gating_grad = jnp.dot(shared.T, logit_low, preferred_element_type=jnp.float32)
    offset_grad = jnp.sum(logit_grad.reshape(row_count, TASKS * EXPERTS), axis=0)
    feature_grad, cross_grad, bias_grad = cross_backward(features, cross_weight, rounded, updates, shared_grad)
    return (task_mixed, feature_grad, grads[0], grads[1], cross_grad, bias_grad, gating_grad, offset_grad)
```

```python
import jax
import jax.numpy as jnp
from jax import lax
from jax.sharding import PartitionSpec as P

F32 = jnp.float32
BF16 = jnp.bfloat16


def cross(features, weight, bias):
    update = jnp.dot(features, weight, preferred_element_type=F32) + bias
    base = features.astype(F32)
    return update, (base * update + base).astype(BF16)


def gating(shared, gate_weight, gate_offset, tasks):
    logits = jnp.dot(shared, gate_weight, preferred_element_type=F32) + gate_offset
    logits = logits.reshape(shared.shape[0], tasks, gate_weight.shape[1] // tasks)
    expo = jnp.exp(logits)
    return expo / jnp.sum(expo, axis=-1, keepdims=True)


def core(features, own_grad, cross_weight, cross_bias, up_weight, down_weight):
    everyone = lax.all_gather(features, "dp", axis=0, tiled=True)
    out_grad = lax.all_gather(own_grad, "dp", axis=0, tiled=True)
    shared = cross(everyone, cross_weight, cross_bias)[1]
    pre = jnp.einsum("rd,edh->reh", shared, up_weight, preferred_element_type=F32)
    sig = jax.nn.sigmoid(pre)
    act = (pre * sig).astype(BF16)
    part = jnp.einsum("reh,ehd->red", act, down_weight, preferred_element_type=F32)
    group_out = lax.psum_scatter(part.astype(BF16), "dp", scatter_dimension=0, tiled=True)
    hidden_grad = jnp.einsum("red,ehd->reh", out_grad, down_weight, preferred_element_type=F32)
    pre_grad = (hidden_grad * sig * (1.0 + pre * (1.0 - sig))).astype(BF16)
    down_grad = jnp.einsum("reh,red->ehd", act, out_grad, preferred_element_type=F32).astype(BF16)
    up_grad = jnp.einsum("rd,reh->edh", shared, pre_grad, preferred_element_type=F32).astype(BF16)
    back = jnp.einsum("reh,edh->rd", pre_grad, up_weight, preferred_element_type=F32)
    return everyone, shared, group_out, down_grad, up_grad, back.astype(BF16)


def local(
    features, cross_weight, cross_bias, gate_weight, gate_offset, up_weight, down_weight, task_grad
):
    rows, tasks, width = task_grad.shape
    exp_dev = up_weight.shape[0]
    rank = lax.axis_index("expert")
    slots = lax.axis_size("expert")
    cols = width // slots
    update, shared_own = cross(features, cross_weight[0], cross_bias[0])
    gates = gating(shared_own, gate_weight, gate_offset, tasks)
    gates_local = lax.dynamic_slice_in_dim(gates, rank * exp_dev, exp_dev, 2)
    wide = task_grad.astype(F32)
    own_grad = sum(
        gates_local[:, t, :, None] * wide[:, t, None, :] for t in range(tasks)
    ).astype(BF16)
    everyone, shared, group_out, down_grad, up_grad, back = core(
        features, own_grad, cross_weight[0], cross_bias[0], up_weight, down_weight
    )
    outs = group_out.astype(F32)
    mixed = sum(gates_local[:, :, e, None] * outs[:, None, e, :] for e in range(exp_dev))
    mixed = lax.psum_scatter(mixed.astype(BF16), "expert", scatter_dimension=0, tiled=True)
    task_mixed = lax.all_gather(mixed, "expert", axis=0, tiled=True)
    gate_part = jnp.stack(
        [jnp.sum(wide * outs[:, None, e, :], axis=-1) for e in range(exp_dev)], axis=-1
    )
    gate_grad = lax.all_gather(gate_part, "expert", axis=2, tiled=True)
    logit_grad = gates * (gate_grad - jnp.sum(gates * gate_grad, axis=-1, keepdims=True))
    logit_flat = logit_grad.reshape(rows, gate_weight.shape[1])
    logit_all = lax.all_gather(logit_flat, "dp", axis=0, tiled=True)
    gating_grad = jnp.dot(shared.T, logit_all.astype(BF16), preferred_element_type=F32)
    offset_grad = jnp.sum(logit_all, axis=0)

    back = lax.psum_scatter(back, "dp", scatter_dimension=0, tiled=True)
    back = lax.psum_scatter(back, "expert", scatter_dimension=1, tiled=True).astype(F32)
    gate_rows = lax.dynamic_slice_in_dim(gate_weight, rank * cols, cols, 0)
    upstream = back + jnp.dot(logit_flat.astype(BF16), gate_rows.T, preferred_element_type=F32)
    base = lax.dynamic_slice_in_dim(features, rank * cols, cols, 1).astype(F32)
    scaled = (upstream * base).astype(BF16)
    scaled_all = lax.all_gather(scaled, "dp", axis=0, tiled=True)
    cross_part = jnp.dot(everyone.T, scaled_all, preferred_element_type=F32)
    bias_part = jnp.sum(scaled_all.astype(F32), axis=0, keepdims=True)
    cross_grad = lax.all_gather(cross_part.astype(BF16), "expert", axis=1, tiled=True).astype(F32)
    bias_grad = lax.all_gather(bias_part, "expert", axis=1, tiled=True)
    upstream = lax.all_gather(upstream, "expert", axis=1, tiled=True)
    scaled = (upstream * features.astype(F32)).astype(BF16)
    feature_grad = (
        upstream
        + jnp.dot(scaled, cross_weight[0].T, preferred_element_type=F32)
        + upstream * update
    ).astype(BF16)
    return (
        task_mixed,
        feature_grad,
        up_grad,
        down_grad,
        cross_grad[None],
        bias_grad,
        gating_grad,
        offset_grad,
    )


def solution(mesh):
    placed = (
        P("dp", None),
        P(),
        P(),
        P(),
        P(),
        P("expert", None, "dp"),
        P("expert", "dp", None),
        P("dp", None, None),
    )
    return jax.shard_map(
        local,
        mesh=mesh,
        in_specs=placed,
        out_specs=(
            P("dp", None, None),
            P("dp", None),
            P("expert", None, "dp"),
            P("expert", "dp", None),
            P(),
            P(),
            P(),
            P(),
        ),
        check_vma=False,
    )
```

```python
import jax
import jax.numpy as jnp
from jax import lax
from jax.experimental import pallas as pl
from jax.experimental.pallas import tpu as pltpu
from jax.sharding import PartitionSpec as P

F32 = jnp.float32
BF16 = jnp.bfloat16


def cross(features, weight, bias):
    update = jnp.dot(features, weight, preferred_element_type=F32) + bias
    base = features.astype(F32)
    return update, (base * update + base).astype(BF16)


def gating(shared, gate_weight, gate_offset, tasks):
    logits = jnp.dot(shared, gate_weight, preferred_element_type=F32) + gate_offset
    logits = logits.reshape(shared.shape[0], tasks, gate_weight.shape[1] // tasks)
    expo = jnp.exp(logits)
    return expo / jnp.sum(expo, axis=-1, keepdims=True)


MESH = pl.DeviceIdType.MESH
THIRDS = ((0, 48), (48, 48), (96, 32))


def place():
    dp, ex = lax.axis_index("dp"), lax.axis_index("expert")
    z, xl, c = dp // 4, lax.rem(dp // 2, 2), lax.rem(dp, 2)

    def rank(dx, dz, core):
        return lax.rem(z + dz + 4, 4) * 4 + (1 - xl if dx else xl) * 2 + core

    return dp, ex, c, rank


class Spread:
    STEPS = (
        ((0, (0, 0)), (1, (0, 0)), (2, (0, 0))),
        ((3, (0, 1)), (4, (0, 1)), (5, (1, 0))),
        ((6, (0, 2)), (7, (1, 1)), (8, (1, -1))),
    )
    GOT = (
        ((0, (1, 0)), (1, (0, 1)), (2, (0, -1))),
        ((3, (1, 1)), (4, (0, 2)), (5, (1, -1))),
        ((6, (1, 2)), (7, (1, 2)), (8, (1, 2))),
    )
    ORDER = ((0, 0), (1, 0), (0, 1), (0, -1), (1, 1), (0, 2), (1, -1), (1, 2))

    def __init__(self, block, own, ssem, rsem):
        self.block, self.own, self.ssem, self.rsem = block, own, ssem, rsem
        self.dp, self.ex, self.c, self.rank = place()
        self.near = (
            self.rank(1, 0, self.c),
            self.rank(0, -1, self.c),
            self.rank(0, 1, self.c),
        )
        self.sent = []

    def copy(self, src, dst, k, to):
        return pltpu.make_async_remote_copy(
            src_ref=src,
            dst_ref=dst,
            send_sem=self.ssem.at[k],
            recv_sem=self.rsem.at[k],
            device_id=(to, self.ex),
            device_id_type=MESH,
        )

    def send(self, step):
        for i, (k, rel) in enumerate(self.STEPS[step]):
            part = THIRDS[i] if step == 2 else (0, 128)
            dst = self.block(self.rank(*rel, self.c), *part)
            src = self.own if step == 0 else dst
            cp = self.copy(src, dst, k, self.near[i])
            cp.start()
            self.sent.append(cp)

    def wait(self, step):
        for i, (k, rel) in enumerate(self.GOT[step]):
            part = THIRDS[i] if step == 2 else (0, 128)
            dst = self.block(self.rank(*rel, self.c), *part)
            self.copy(dst, dst, k, self.near[i]).wait_recv()

    def share(self, lo, hi):
        for j in range(lo, hi):
            dst = self.block(self.rank(*self.ORDER[j], self.c), 0, 128)
            cp = self.copy(self.own if j == 0 else dst, dst, 9 + j, self.rank(0, 0, 1 - self.c))
            cp.start()
            self.sent.append(cp)

    def wait_shared(self):
        for j in range(8):
            dst = self.block(self.rank(*self.ORDER[j], 1 - self.c), 0, 128)
            self.copy(dst, dst, 9 + j, self.rank(0, 0, 1 - self.c)).wait_recv()

    def drain(self):
        for cp in self.sent:
            cp.wait_send()


class Gather:
    def __init__(self, part, ra, rb, rc, ssem, rsem):
        self.part, self.ra, self.rb, self.rc = part, ra, rb, rc
        self.ssem, self.rsem = ssem, rsem
        self.dp, self.ex, self.c, self.rank = place()
        self.x = self.rank(1, 0, self.c)
        self.up = self.rank(0, 1, self.c)
        self.down = self.rank(0, -1, self.c)
        self.sent = []

    def ref(self, dx, dz):
        return self.part.at[self.rank(dx, dz, 0) // 2, self.c]

    def copy(self, src, dst, k, to):
        return pltpu.make_async_remote_copy(
            src_ref=src,
            dst_ref=dst,
            send_sem=self.ssem.at[k],
            recv_sem=self.rsem.at[k],
            device_id=(to, self.ex),
            device_id_type=MESH,
        )

    def go(self, src, dst, k, to):
        cp = self.copy(src, dst, k, to)
        cp.start()
        self.sent.append(cp)

    def add(self, ref, got):
        ref[...] = (ref[...].astype(F32) + got[...].astype(F32)).astype(BF16)

    def send_a(self):
        for i, to in enumerate((self.x, self.up, self.down)):
            rows = pl.ds(*THIRDS[i])
            self.go(self.ref(1, 2).at[rows], self.ra.at[rows], i, to)

    def wait_a(self):
        for i, rel in enumerate(((0, 2), (1, 1), (1, -1))):
            rows = pl.ds(*THIRDS[i])
            got = self.ra.at[rows]
            self.copy(got, got, i, self.x).wait_recv()
            self.add(self.ref(*rel).at[rows], got)

    def send_b(self):
        self.go(self.ref(1, 1), self.rb.at[1], 4, self.x)
        self.go(self.ref(0, 2), self.rb.at[0], 3, self.up)
        self.go(self.ref(1, -1), self.rb.at[2], 5, self.down)

    def wait_b(self):
        for i, rel in enumerate(((0, 1), (0, 1), (1, 0))):
            got = self.rb.at[i]
            self.copy(got, got, 3 + i, self.x).wait_recv()
            self.add(self.ref(*rel), got)

    def send_c(self):
        self.go(self.ref(1, 0), self.rc.at[0], 6, self.x)
        self.go(self.ref(0, 1), self.rc.at[1], 7, self.up)
        self.go(self.ref(0, -1), self.rc.at[2], 8, self.down)

    def wait_c(self):
        total = self.ref(0, 0)[...].astype(F32)
        for i in range(3):
            got = self.rc.at[i]
            self.copy(got, got, 6 + i, self.x).wait_recv()
            total = total + got[...].astype(F32)
        return total

    def drain(self):
        for cp in self.sent:
            cp.wait_send()


def dot(a, b, dims):
    return lax.dot_general(a, b, (dims, ((), ())), preferred_element_type=F32)


NN, NT, TN = ((1,), (0,)), ((1,), (1,)), ((0,), (0,))


def expert_kernel(
    feat_in, og_in, wc_in, bias_in, up_in, down_in,
    feat_out, shared_out, group_out, dgrad_out, ugrad_out, back_out,
    feat, shared, og, wc, up, down, act, dsl, part, crecv, ra, rb, rc, group, stage_d, stage_u,
    load_sem, out_sem, stage_sem, fs, fr, gs, gr, cs, cr, ts, tr,
):
    dp, ex, c, rank = place()
    barrier = pltpu.get_barrier_semaphore()
    for to in (rank(1, 0, c), rank(0, 1, c), rank(0, -1, c), rank(0, 0, 1 - c)):
        pl.semaphore_signal(barrier, inc=1, device_id=(to, ex), device_id_type=MESH)
    loads = [
        pltpu.make_async_copy(src, dst, load_sem.at[i])
        for i, (src, dst) in enumerate((
            (feat_in, feat.at[pl.ds(dp * 128, 128)]),
            (og_in, og.at[:, pl.ds(dp * 128, 128)]),
            (wc_in, wc), (up_in, up), (down_in, down),
        ))
    ]
    for cp in loads:
        cp.start()
    pl.semaphore_wait(barrier, 4)
    first = Spread(lambda d, r, n: feat.at[pl.ds(d * 128 + r, n)], feat_in, fs, fr)
    second = Spread(lambda d, r, n: og.at[:, pl.ds(d * 128 + r, n)], og_in, gs, gr)
    first.send(0)
    first.wait(0)
    first.send(1)
    first.share(0, 4)
    second.send(0)
    first.wait(1)
    first.send(2)
    first.share(4, 7)
    for cp in loads:
        cp.wait()
    first.wait(2)
    first.share(7, 8)
    first.wait_shared()

    def hidden(k, carry):
        rows = pl.ds(pl.multiple_of(k * 256, 256), 256)
        for n in range(2):
            cols = pl.ds(n * 512, 512)
            base = feat[rows, cols].astype(F32)
            update = dot(feat[rows, :], wc[:, cols], NN) + bias_in[:, cols]
            shared[rows, cols] = (base * update + base).astype(BF16)
        for e in range(2):
            pre = dot(shared[rows, :], up[e], NN)
            sig = jax.nn.sigmoid(pre)
            act[e, rows] = (pre * sig).astype(BF16)
            dsl[e, rows] = (sig * (1.0 + pre * (1.0 - sig))).astype(BF16)
        return carry

    lax.fori_loop(0, 4, hidden, 0)
    second.wait(0)
    second.send(1)
    second.share(0, 4)
    lax.fori_loop(4, 8, hidden, 0)
    outs = [
        pltpu.make_async_copy(feat, feat_out, out_sem.at[0]),
        pltpu.make_async_copy(shared, shared_out, out_sem.at[1]),
    ]
    for cp in outs:
        cp.start()

    swaps = []
    trees = []
    for e in range(2):
        def forward(k, carry):
            rows = pl.ds(pl.multiple_of(k * 256, 256), 256)
            for n in range(2):
                cols = pl.ds(n * 512, 512)
                out = dot(act[e, rows], down[e, :, cols], NN).astype(BF16)
                part[e, k, 0, :, cols] = out[:128]
                part[e, k, 1, :, cols] = out[128:]
            return carry

        lax.fori_loop(0, 8, forward, 0)
        if e == 0:
            second.wait(1)
            second.send(2)
            second.share(4, 7)
        swap = pltpu.make_async_remote_copy(
            src_ref=part.at[e, :, 1 - c],
            dst_ref=crecv.at[e],
            send_sem=cs.at[e],
            recv_sem=cr.at[e],
            device_id=(rank(0, 0, 1 - c), ex),
            device_id_type=MESH,
        )
        swap.start()
        swaps.append(swap)
        trees.append(Gather(part.at[e], ra.at[e], rb.at[e], rc.at[e], ts.at[e], tr.at[e]))
    second.wait(2)
    second.share(7, 8)
    for e in range(2):
        swaps[e].wait_recv()

        def merge(k, carry):
            part[e, k, c] = (part[e, k, c].astype(F32) + crecv[e, k].astype(F32)).astype(BF16)
            return carry

        lax.fori_loop(0, 8, merge, 0)
        trees[e].send_a()
    for e in range(2):
        trees[e].wait_a()
        trees[e].send_b()
    second.wait_shared()

    for e in range(2):
        def backward(k, carry):
            rows = pl.ds(pl.multiple_of(k * 256, 256), 256)
            grad = dot(og[e, rows], down[e], NT)
            dsl[e, rows] = (grad * dsl[e, rows].astype(F32)).astype(BF16)
            return carry

        lax.fori_loop(0, 8, backward, 0)
        trees[e].wait_b()
        trees[e].send_c()
    for e in range(2):
        swaps[e].wait_send()

    def to_shared(k, carry):
        rows = pl.ds(pl.multiple_of(k * 256, 256), 256)
        for n in range(2):
            cols = pl.ds(n * 512, 512)
            grad = dot(dsl[0, rows], up[0, cols], NT) + dot(dsl[1, rows], up[1, cols], NT)
            crecv[0, k, :, cols] = grad[:128].astype(BF16)
            crecv[1, k, :, cols] = grad[128:].astype(BF16)
        return carry

    lax.fori_loop(0, 8, to_shared, 0)
    for core in range(2):
        cp = pltpu.make_async_copy(crecv.at[core], back_out.at[:, core], out_sem.at[2 + core])
        cp.start()
        outs.append(cp)
    for e in range(2):
        group[e] = trees[e].wait_c()
    cp = pltpu.make_async_copy(group, group_out, out_sem.at[4])
    cp.start()
    outs.append(cp)

    for e in range(2):
        def weight(m, carry):
            cols = pl.ds(pl.multiple_of(m * 256, 256), 256)
            stage_d[e, cols] = dot(act[e, :, cols], og[e], TN).astype(BF16)
            return carry

        lax.fori_loop(0, 2, weight, 0)
    cp = pltpu.make_async_copy(stage_d, dgrad_out, stage_sem.at[0])
    cp.start()
    outs.append(cp)

    def weight_up(m, carry):
        cols = pl.ds(pl.multiple_of(m * 256, 256), 256)
        for e in range(2):
            stage_u[e, cols] = dot(shared[:, cols], dsl[e], TN).astype(BF16)
        return carry

    lax.fori_loop(0, 4, weight_up, 0)
    cp = pltpu.make_async_copy(stage_u, ugrad_out, stage_sem.at[1])
    cp.start()
    outs.append(cp)
    first.drain()
    second.drain()
    for tree in trees:
        tree.drain()
    for cp in outs:
        cp.wait()


def core(features, own_grad, cross_weight, cross_bias, up_weight, down_weight):
    rows, width = features.shape
    exp_dev, _, hid = up_weight.shape
    group = 16
    every = group * rows
    anywhere = pl.BlockSpec(memory_space=pl.ANY)
    inside = pl.BlockSpec(memory_space=pltpu.VMEM)
    dma = pltpu.SemaphoreType.DMA
    outs = pl.pallas_call(
        expert_kernel,
        out_shape=(
            jax.ShapeDtypeStruct((every, width), BF16),
            jax.ShapeDtypeStruct((every, width), BF16),
            jax.ShapeDtypeStruct((exp_dev, rows, width), F32),
            jax.ShapeDtypeStruct(down_weight.shape, BF16),
            jax.ShapeDtypeStruct(up_weight.shape, BF16),
            jax.ShapeDtypeStruct((8, 2, rows, width), BF16),
        ),
        in_specs=[inside, inside, anywhere, inside, anywhere, anywhere],
        out_specs=[anywhere] * 6,
        scratch_shapes=[
            pltpu.VMEM((every, width), BF16),
            pltpu.VMEM((every, width), BF16),
            pltpu.VMEM((exp_dev, every, width), BF16),
            pltpu.VMEM((width, width), BF16),
            pltpu.VMEM(up_weight.shape, BF16),
            pltpu.VMEM(down_weight.shape, BF16),
            pltpu.VMEM((exp_dev, every, hid), BF16),
            pltpu.VMEM((exp_dev, every, hid), BF16),
            pltpu.VMEM((exp_dev, 8, 2, rows, width), BF16),
            pltpu.VMEM((exp_dev, 8, rows, width), BF16),
            pltpu.VMEM((exp_dev, rows, width), BF16),
            pltpu.VMEM((exp_dev, 3, rows, width), BF16),
            pltpu.VMEM((exp_dev, 3, rows, width), BF16),
            pltpu.VMEM((exp_dev, rows, width), F32),
            pltpu.VMEM(down_weight.shape, BF16),
            pltpu.VMEM(up_weight.shape, BF16),
            dma((5,)), dma((5,)), dma((2,)),
            dma((17,)), dma((17,)), dma((17,)), dma((17,)),
            dma((2,)), dma((2,)), dma((2, 9)), dma((2, 9)),
        ],
        compiler_params=pltpu.CompilerParams(
            collective_id=0, has_side_effects=True, vmem_limit_bytes=67043328
        ),
        name="experts",
    )(features, own_grad, cross_weight, cross_bias, up_weight, down_weight)
    everyone, shared, group_out, down_grad, up_grad, back = outs
    return everyone, shared, group_out, down_grad, up_grad, back.reshape(every, width)


def local(
    features, cross_weight, cross_bias, gate_weight, gate_offset, up_weight, down_weight, task_grad
):
    rows, tasks, width = task_grad.shape
    exp_dev = up_weight.shape[0]
    rank = lax.axis_index("expert")
    slots = lax.axis_size("expert")
    cols = width // slots
    update, shared_own = cross(features, cross_weight[0], cross_bias[0])
    gates = gating(shared_own, gate_weight, gate_offset, tasks)
    gates_local = lax.dynamic_slice_in_dim(gates, rank * exp_dev, exp_dev, 2)
    wide = task_grad.astype(F32)
    own_grad = jnp.stack(
        [sum(gates_local[:, t, e, None] * wide[:, t] for t in range(tasks)) for e in range(exp_dev)]
    ).astype(BF16)
    everyone, shared, group_out, down_grad, up_grad, back = core(
        features, own_grad, cross_weight[0], cross_bias, up_weight, down_weight
    )
    mixed = sum(gates_local[:, :, e, None] * group_out[e, :, None, :] for e in range(exp_dev))
    mixed = lax.psum_scatter(mixed.astype(BF16), "expert", scatter_dimension=0, tiled=True)
    task_mixed = lax.all_gather(mixed, "expert", axis=0, tiled=True)
    gate_part = jnp.stack(
        [jnp.sum(wide * group_out[e, :, None, :], axis=-1) for e in range(exp_dev)], axis=-1
    )
    gate_grad = lax.all_gather(gate_part, "expert", axis=2, tiled=True)
    logit_grad = gates * (gate_grad - jnp.sum(gates * gate_grad, axis=-1, keepdims=True))
    logit_flat = logit_grad.reshape(rows, gate_weight.shape[1])
    logit_all = lax.all_gather(logit_flat, "dp", axis=0, tiled=True)
    gating_grad = jnp.dot(shared.T, logit_all.astype(BF16), preferred_element_type=F32)
    offset_grad = jnp.sum(logit_all, axis=0)

    back = lax.psum_scatter(back, "dp", scatter_dimension=0, tiled=True)
    back = lax.psum_scatter(back, "expert", scatter_dimension=1, tiled=True).astype(F32)
    gate_rows = lax.dynamic_slice_in_dim(gate_weight, rank * cols, cols, 0)
    upstream = back + jnp.dot(logit_flat.astype(BF16), gate_rows.T, preferred_element_type=F32)
    base = lax.dynamic_slice_in_dim(features, rank * cols, cols, 1).astype(F32)
    scaled = (upstream * base).astype(BF16)
    scaled_all = lax.all_gather(scaled, "dp", axis=0, tiled=True)
    cross_part = jnp.dot(everyone.T, scaled_all, preferred_element_type=F32)
    bias_part = jnp.sum(scaled_all.astype(F32), axis=0, keepdims=True)
    cross_grad = lax.all_gather(cross_part.astype(BF16), "expert", axis=1, tiled=True).astype(F32)
    bias_grad = lax.all_gather(bias_part, "expert", axis=1, tiled=True)
    upstream = lax.all_gather(upstream, "expert", axis=1, tiled=True)
    scaled = (upstream * features.astype(F32)).astype(BF16)
    feature_grad = (
        upstream
        + jnp.dot(scaled, cross_weight[0].T, preferred_element_type=F32)
        + upstream * update
    ).astype(BF16)
    return (
        task_mixed,
        feature_grad,
        up_grad,
        down_grad,
        cross_grad[None],
        bias_grad,
        gating_grad,
        offset_grad,
    )


def solution(mesh):
    placed = (
        P("dp", None),
        P(),
        P(),
        P(),
        P(),
        P("expert", None, "dp"),
        P("expert", "dp", None),
        P("dp", None, None),
    )
    return jax.shard_map(
        local,
        mesh=mesh,
        in_specs=placed,
        out_specs=(
            P("dp", None, None),
            P("dp", None),
            P("expert", None, "dp"),
            P("expert", "dp", None),
            P(),
            P(),
            P(),
            P(),
        ),
        check_vma=False,
    )
```

```python
import jax
import jax.numpy as jnp
from jax import lax
from jax.experimental import pallas as pl
from jax.experimental.pallas import tpu as pltpu
from jax.sharding import PartitionSpec as P

F32 = jnp.float32
BF16 = jnp.bfloat16


def cross(features, weight, bias):
    update = jnp.dot(features, weight, preferred_element_type=F32) + bias
    base = features.astype(F32)
    return update, (base * update + base).astype(BF16)


def gating(shared, gate_weight, gate_offset, tasks):
    logits = jnp.dot(shared, gate_weight, preferred_element_type=F32) + gate_offset
    logits = logits.reshape(shared.shape[0], tasks, gate_weight.shape[1] // tasks)
    expo = jnp.exp(logits)
    return expo / jnp.sum(expo, axis=-1, keepdims=True)


MESH = pl.DeviceIdType.MESH
THIRDS = ((0, 48), (48, 48), (96, 32))


def place():
    dp, ex = lax.axis_index("dp"), lax.axis_index("expert")
    z, xl, c = dp // 4, lax.rem(dp // 2, 2), lax.rem(dp, 2)

    def rank(dx, dz, core):
        return lax.rem(z + dz + 4, 4) * 4 + (1 - xl if dx else xl) * 2 + core

    return dp, ex, c, rank


class Spread:
    STEPS = (
        ((0, (0, 0)), (1, (0, 0)), (2, (0, 0))),
        ((3, (0, 1)), (4, (0, 1)), (5, (1, 0))),
        ((6, (0, 2)), (7, (1, 1)), (8, (1, -1))),
    )
    GOT = (
        ((0, (1, 0)), (1, (0, 1)), (2, (0, -1))),
        ((3, (1, 1)), (4, (0, 2)), (5, (1, -1))),
        ((6, (1, 2)), (7, (1, 2)), (8, (1, 2))),
    )
    ORDER = ((0, 0), (1, 0), (0, 1), (0, -1), (1, 1), (0, 2), (1, -1), (1, 2))

    def __init__(self, block, own, ssem, rsem):
        self.block, self.own, self.ssem, self.rsem = block, own, ssem, rsem
        self.dp, self.ex, self.c, self.rank = place()
        self.near = (
            self.rank(1, 0, self.c),
            self.rank(0, -1, self.c),
            self.rank(0, 1, self.c),
        )
        self.sent = []

    def copy(self, src, dst, k, to):
        return pltpu.make_async_remote_copy(
            src_ref=src,
            dst_ref=dst,
            send_sem=self.ssem.at[k],
            recv_sem=self.rsem.at[k],
            device_id=(to, self.ex),
            device_id_type=MESH,
        )

    def send(self, step):
        for i, (k, rel) in enumerate(self.STEPS[step]):
            part = THIRDS[i] if step == 2 else (0, 128)
            dst = self.block(self.rank(*rel, self.c), *part)
            src = self.own if step == 0 else dst
            cp = self.copy(src, dst, k, self.near[i])
            cp.start()
            self.sent.append(cp)

    def wait(self, step):
        for i, (k, rel) in enumerate(self.GOT[step]):
            part = THIRDS[i] if step == 2 else (0, 128)
            dst = self.block(self.rank(*rel, self.c), *part)
            self.copy(dst, dst, k, self.near[i]).wait_recv()

    def share(self, lo, hi):
        for j in range(lo, hi):
            dst = self.block(self.rank(*self.ORDER[j], self.c), 0, 128)
            cp = self.copy(self.own if j == 0 else dst, dst, 9 + j, self.rank(0, 0, 1 - self.c))
            cp.start()
            self.sent.append(cp)

    def wait_shared(self):
        for j in range(8):
            dst = self.block(self.rank(*self.ORDER[j], 1 - self.c), 0, 128)
            self.copy(dst, dst, 9 + j, self.rank(0, 0, 1 - self.c)).wait_recv()

    def drain(self):
        for cp in self.sent:
            cp.wait_send()


class Gather:
    def __init__(self, block, ra, rb, rc, ssem, rsem):
        self.block, self.ra, self.rb, self.rc = block, ra, rb, rc
        self.ssem, self.rsem = ssem, rsem
        self.dp, self.ex, self.c, self.rank = place()
        self.x = self.rank(1, 0, self.c)
        self.up = self.rank(0, 1, self.c)
        self.down = self.rank(0, -1, self.c)
        self.sent = []

    def ref(self, dx, dz):
        return self.block(self.rank(dx, dz, 0) // 2)

    def copy(self, src, dst, k, to):
        return pltpu.make_async_remote_copy(
            src_ref=src,
            dst_ref=dst,
            send_sem=self.ssem.at[k],
            recv_sem=self.rsem.at[k],
            device_id=(to, self.ex),
            device_id_type=MESH,
        )

    def go(self, src, dst, k, to):
        cp = self.copy(src, dst, k, to)
        cp.start()
        self.sent.append(cp)

    def add(self, ref, got):
        ref[...] = (ref[...].astype(F32) + got[...].astype(F32)).astype(BF16)

    def send_a(self):
        for i, to in enumerate((self.x, self.up, self.down)):
            rows = pl.ds(*THIRDS[i])
            self.go(self.ref(1, 2).at[rows], self.ra.at[rows], i, to)

    def wait_a(self):
        for i, rel in enumerate(((0, 2), (1, 1), (1, -1))):
            rows = pl.ds(*THIRDS[i])
            got = self.ra.at[rows]
            self.copy(got, got, i, self.x).wait_recv()
            self.add(self.ref(*rel).at[rows], got)

    def send_b(self):
        self.go(self.ref(1, 1), self.rb.at[1], 4, self.x)
        self.go(self.ref(0, 2), self.rb.at[0], 3, self.up)
        self.go(self.ref(1, -1), self.rb.at[2], 5, self.down)

    def wait_b(self):
        for i, rel in enumerate(((0, 1), (0, 1), (1, 0))):
            got = self.rb.at[i]
            self.copy(got, got, 3 + i, self.x).wait_recv()
            self.add(self.ref(*rel), got)

    def send_c(self):
        self.go(self.ref(1, 0), self.rc.at[0], 6, self.x)
        self.go(self.ref(0, 1), self.rc.at[1], 7, self.up)
        self.go(self.ref(0, -1), self.rc.at[2], 8, self.down)

    def wait_c(self):
        total = self.ref(0, 0)[...].astype(F32)
        for i in range(3):
            got = self.rc.at[i]
            self.copy(got, got, 6 + i, self.x).wait_recv()
            total = total + got[...].astype(F32)
        return total

    def drain(self):
        for cp in self.sent:
            cp.wait_send()


class Sides:
    def __init__(self, ref, ssem, rsem):
        self.ref, self.ssem, self.rsem = ref, ssem, rsem
        self.dp, ex = lax.axis_index("dp"), lax.axis_index("expert")
        self.y, self.h = lax.rem(ex, 4), ex // 4
        self.other = (1 - self.h) * 4 + self.y
        self.up = self.h * 4 + lax.rem(self.y + 1, 4)
        self.down = self.h * 4 + lax.rem(self.y + 3, 4)
        self.sent = []

    def at(self, dy, h):
        return self.ref(lax.rem(self.y + dy + 4, 4), h)

    def copy(self, src, dst, k, to):
        return pltpu.make_async_remote_copy(
            src_ref=src,
            dst_ref=dst,
            send_sem=self.ssem.at[k],
            recv_sem=self.rsem.at[k],
            device_id=(self.dp, to),
            device_id_type=MESH,
        )

    def go(self, src, dst, k, to):
        cp = self.copy(src, dst, k, to)
        cp.start()
        self.sent.append(cp)

    def got(self, dst, k):
        self.copy(dst, dst, k, self.other).wait_recv()

    def drain(self):
        for cp in self.sent:
            cp.wait_send()


class Wide(Sides):
    def send_x(self):
        self.go(self.at(0, self.h), self.at(0, self.h), 0, self.other)

    def wait_x(self):
        self.got(self.at(0, 1 - self.h), 0)

    def send_a(self):
        for h in range(2):
            self.go(self.at(0, h), self.at(0, h), 1 + h, self.down)
            self.go(self.at(0, h), self.at(0, h), 3 + h, self.up)

    def wait_a(self):
        for h in range(2):
            self.got(self.at(1, h), 1 + h)
            self.got(self.at(-1, h), 3 + h)

    def send_b(self):
        self.go(self.at(1, 0), self.at(1, 0), 5, self.down)
        self.go(self.at(-1, 1), self.at(-1, 1), 6, self.up)

    def wait_b(self):
        for h in range(2):
            self.got(self.at(2, h), 5 + h)


class Narrow(Sides):
    def __init__(self, ref, ra, rb, ssem, rsem):
        super().__init__(ref, ssem, rsem)
        self.ra, self.rb = ra, rb

    def send_a(self):
        self.go(self.at(2, 0), self.ra.at[0], 0, self.up)
        self.go(self.at(2, 1), self.ra.at[1], 1, self.down)

    def wait_a(self):
        for h, dy in enumerate((1, -1)):
            self.got(self.ra.at[h], h)
            ref, got = self.at(dy, h), self.ra.at[h]

            def add(k, carry):
                ref[k] = (ref[k].astype(F32) + got[k].astype(F32)).astype(BF16)
                return carry

            lax.fori_loop(0, got.shape[0], add, 0)

    def send_b(self):
        for h in range(2):
            self.go(self.at(1, h), self.rb.at[0, h], 2 + h, self.up)
            self.go(self.at(-1, h), self.rb.at[1, h], 4 + h, self.down)

    def wait_b(self, put):
        for h in range(2):
            for d in range(2):
                self.got(self.rb.at[d, h], 2 + 2 * d + h)
            ref = self.at(0, h)

            def add(k, carry):
                total = ref[k].astype(F32) + self.rb[0, h, k].astype(F32)
                put(k, h, (total + self.rb[1, h, k].astype(F32)).astype(BF16))
                return carry

            lax.fori_loop(0, ref.shape[0], add, 0)


class Push:
    def __init__(self, axis, slot, ssem, rsem):
        self.slot, self.ssem, self.rsem = slot, ssem, rsem
        self.n, self.me = lax.axis_size(axis), lax.axis_index(axis)
        if axis == "dp":
            other = lax.axis_index("expert")
            self.to = lambda k: (k, other)
        else:
            other = lax.axis_index("dp")
            self.to = lambda k: (other, k)
        self.sent = []

    def copy(self, i, k, to):
        return pltpu.make_async_remote_copy(
            src_ref=self.slot(i),
            dst_ref=self.slot(i),
            send_sem=self.ssem.at[k - 1],
            recv_sem=self.rsem.at[k - 1],
            device_id=self.to(to),
            device_id_type=MESH,
        )

    def send(self):
        for k in range(1, self.n):
            cp = self.copy(self.me, k, lax.rem(self.me + k, self.n))
            cp.start()
            self.sent.append(cp)

    def wait(self):
        for k in range(1, self.n):
            source = lax.rem(self.me + self.n - k, self.n)
            self.copy(source, k, source).wait_recv()

    def drain(self):
        for cp in self.sent:
            cp.wait_send()


def dot(a, b, dims):
    return lax.dot_general(a, b, (dims, ((), ())), preferred_element_type=F32)


NN, NT, TN = ((1,), (0,)), ((1,), (1,)), ((0,), (0,))


def expert_kernel(
    feat_in, og_in, wc_in, bias_in, up_in, down_in, tg, gates_all, gates_own, gate_w,
    mixed_out, fgrad_out, ugrad_out, dgrad_out, cross_out, bias_out, gating_out, offset_out,
    feat, shared, og, wc, up, down, act, dsl, part, crecv, ra, rb, rc, group,
    mix, mra, mrb, mrx, tmx, bra, brb, bt, ta, tb, tc, bh, bx, gp, lall, gx, dall, crs, biases,
    cst, gf, dus, fgs, gts, bst, ost,
    load_sem, out_sem, wgrad_sem, cst_sem, fs, fr, gs, gr, cs, cr, ts, tr,
    ms, mr, ws, wr, bs, br, us, ur, xs, xr, ps, pr, ls, lr, hs, hr, ds, dr, vs, vr, ks, kr, zs, zr,
    free,
):
    dp, ex, c, rank = place()
    barrier = pltpu.get_barrier_semaphore()
    for k in range(1, 16):
        to = (lax.rem(dp + k, 16), ex)
        pl.semaphore_signal(barrier, inc=1, device_id=to, device_id_type=MESH)
    for k in range(1, 8):
        to = (dp, lax.rem(ex + k, 8))
        pl.semaphore_signal(barrier, inc=1, device_id=to, device_id_type=MESH)
    loads = [
        pltpu.make_async_copy(src, dst, load_sem.at[i])
        for i, (src, dst) in enumerate((
            (feat_in, feat.at[pl.ds(dp * 128, 128)]),
            (og_in, og.at[:, pl.ds(dp * 128, 128)]),
            (wc_in, wc), (up_in, up), (down_in, down),
        ))
    ]
    for cp in loads:
        cp.start()
    pl.semaphore_wait(barrier, 22)
    first = Spread(lambda d, r, n: feat.at[pl.ds(d * 128 + r, n)], feat_in, fs, fr)
    second = Spread(lambda d, r, n: og.at[:, pl.ds(d * 128 + r, n)], og_in, gs, gr)
    first.send(0)
    first.wait(0)
    first.send(1)
    first.share(0, 4)
    second.send(0)
    first.wait(1)
    first.send(2)
    first.share(4, 7)
    for cp in loads:
        cp.wait()
    first.wait(2)
    first.share(7, 8)
    first.wait_shared()

    def hidden(k, carry):
        rows = pl.ds(pl.multiple_of(k * 256, 256), 256)
        for n in range(2):
            cols = pl.ds(n * 512, 512)
            base = feat[rows, cols].astype(F32)
            update = dot(feat[rows, :], wc[:, cols], NN) + bias_in[:, cols]
            shared[rows, cols] = (base * update + base).astype(BF16)
        for e in range(2):
            pre = dot(shared[rows, :], up[e], NN)
            sig = jax.nn.sigmoid(pre)
            act[e, rows] = (pre * sig).astype(BF16)
            dsl[e, rows] = (sig * (1.0 + pre * (1.0 - sig))).astype(BF16)
        return carry

    lax.fori_loop(0, 4, hidden, 0)
    second.wait(0)
    second.send(1)
    second.share(0, 4)
    lax.fori_loop(4, 8, hidden, 0)
    outs = []
    partner = (rank(0, 0, 1 - c), ex)

    swaps = []
    trees = []
    for e in range(2):
        def forward(k, carry):
            rows = pl.ds(pl.multiple_of(k * 256, 256), 256)
            for n in range(2):
                cols = pl.ds(n * 512, 512)
                out = dot(act[e, rows], down[e, :, cols], NN).astype(BF16)
                part[e, k, 0, :, cols] = out[:128]
                part[e, k, 1, :, cols] = out[128:]
            return carry

        lax.fori_loop(0, 8, forward, 0)
        if e == 0:
            second.wait(1)
            second.send(2)
            second.share(4, 7)
        swap = pltpu.make_async_remote_copy(
            src_ref=part.at[e, :, 1 - c],
            dst_ref=crecv.at[e],
            send_sem=cs.at[e],
            recv_sem=cr.at[e],
            device_id=partner,
            device_id_type=MESH,
        )
        swap.start()
        swaps.append(swap)
        blocks = lambda k, e=e: part.at[e, k, c]
        trees.append(Gather(blocks, ra.at[e], rb.at[e], rc.at[e], ts.at[e], tr.at[e]))
    second.wait(2)
    second.share(7, 8)
    for e in range(2):
        swaps[e].wait_recv()

        def merge(k, carry):
            part[e, k, c] = (part[e, k, c].astype(F32) + crecv[e, k].astype(F32)).astype(BF16)
            return carry

        lax.fori_loop(0, 8, merge, 0)
        if e == 0:
            pl.semaphore_signal(free, inc=1, device_id=partner, device_id_type=MESH)
        trees[e].send_a()
    for e in range(2):
        trees[e].wait_a()
        trees[e].send_b()
    second.wait_shared()

    for e in range(2):
        def backward(k, carry):
            rows = pl.ds(pl.multiple_of(k * 256, 256), 256)
            grad = dot(og[e, rows], down[e], NT)
            dsl[e, rows] = (grad * dsl[e, rows].astype(F32)).astype(BF16)
            return carry

        lax.fori_loop(0, 8, backward, 0)
        trees[e].wait_b()
        trees[e].send_c()
    for e in range(2):
        swaps[e].wait_send()

    def to_shared(k, carry):
        rows = pl.ds(pl.multiple_of(k * 256, 256), 256)
        for n in range(2):
            cols = pl.ds(n * 512, 512)
            grad = dot(dsl[0, rows], up[0, cols], NT) + dot(dsl[1, rows], up[1, cols], NT)
            part[1 - c, k, 1 - c, :, cols] = grad[:128].astype(BF16)
            part[c, k, 1 - c, :, cols] = grad[128:].astype(BF16)
        return carry

    lax.fori_loop(0, 8, to_shared, 0)
    pl.semaphore_wait(free, 1)
    swap = pltpu.make_async_remote_copy(
        src_ref=part.at[0, :, 1 - c],
        dst_ref=crecv.at[0],
        send_sem=cs.at[2],
        recv_sem=cr.at[2],
        device_id=partner,
        device_id_type=MESH,
    )
    swap.start()
    for e in range(2):
        group[e] = trees[e].wait_c()

    y, high = lax.rem(ex, 4), ex // 4
    pos = y * 2 + high
    own = pl.ds(pl.multiple_of(dp * 128, 128), 128)
    own_cols = pl.ds(pl.multiple_of(pos * 128, 128), 128)
    lane = lax.broadcasted_iota(jnp.int32, (128, 128), 1)
    packed = jnp.zeros((128, 128), F32)
    for e in range(2):
        for t in range(4):
            inner = jnp.sum(tg[t].astype(F32) * group[e], axis=1, keepdims=True)
            packed = packed + jnp.where(lane == e * 4 + t, inner, 0.0)
    gp[ex] = packed.T[:8]
    parts = Push("expert", lambda i: gp.at[i], ps, pr)
    parts.send()
    for t in range(4):
        mix[t] = (
            gates_own[:, t : t + 1] * group[0] + gates_own[:, t + 4 : t + 5] * group[1]
        ).astype(BF16)
    mixer = Narrow(
        lambda yp, h: mix.at[:, pl.ds(pl.multiple_of(yp * 32 + h * 16, 16), 16)], mra, mrb, ms, mr
    )
    mixer.send_a()
    swap.wait_recv()

    def merge_back(k, carry):
        total = part[1, k, 1 - c].astype(F32) + crecv[0, k].astype(F32)
        part[1, k, 1 - c] = total.astype(BF16)
        return carry

    lax.fori_loop(0, 8, merge_back, 0)
    back = Narrow(
        lambda yp, h: part.at[1, :, 1 - c, :, pl.ds(pl.multiple_of(yp * 256 + h * 128, 128), 128)],
        bra, brb, bs, br,
    )
    back.send_a()
    for tree in trees:
        tree.drain()

    def weight_down(i, carry):
        e, m = i // 2, lax.rem(i, 2)
        cols = pl.ds(pl.multiple_of(m * 256, 256), 256)
        tile = dot(act[e, :, cols], og[e], TN).astype(BF16)
        part[0, i * 2, c] = tile[:128]
        part[0, i * 2 + 1, c] = tile[128:]
        return carry

    def weight_up(m, carry):
        cols = pl.ds(pl.multiple_of(m * 256, 256), 256)
        for e in range(2):
            tile = dot(shared[:, cols], dsl[e], TN).astype(BF16)
            part[1, e * 4 + m, c, :, :512] = tile[:128]
            part[1, e * 4 + m, c, :, 512:] = tile[128:]
        return carry

    lax.fori_loop(0, 2, weight_down, 0)
    mixer.wait_a()
    mixer.send_b()
    lax.fori_loop(2, 4, weight_down, 0)
    back.wait_a()
    back.send_b()
    for i in range(8):
        dst = dgrad_out.at[i // 4, pl.ds(i % 4 * 128, 128)]
        cp = pltpu.make_async_copy(part.at[0, i, c], dst, wgrad_sem.at[i])
        cp.start()
        outs.append(cp)

    parts.wait()
    weighed = [gates_all[i] * gp[i] for i in range(8)]
    total = sum(weighed[1:], weighed[0])
    total = total + pltpu.roll(total, 4, 0)
    for i in range(8):
        lall[pl.ds(i * 8, 8), own] = gates_all[i] * (gp[i] - total)
    logits = Push("dp", lambda i: lall.at[:, pl.ds(pl.multiple_of(i * 128, 128), 128)], ls, lr)
    logits.send()

    def keep_mix(k, h, total):
        mix[k, pl.ds(pl.multiple_of(y * 32 + h * 16, 16), 16)] = total

    mixer.wait_b(keep_mix)
    cross_mix = pltpu.make_async_remote_copy(
        src_ref=mixer.at(0, 1 - high),
        dst_ref=mrx,
        send_sem=xs.at[0],
        recv_sem=xr.at[0],
        device_id=(dp, (1 - high) * 4 + y),
        device_id_type=MESH,
    )
    cross_mix.start()
    lax.fori_loop(0, 2, weight_up, 0)

    def keep_back(k, h, total):
        bt[k, :, pl.ds(h * 128, 128)] = total

    back.wait_b(keep_back)
    tree = Gather(lambda k: bt.at[k], ta, tb, tc, us, ur)
    tree.send_a()
    cross_mix.wait_recv()
    mine = pl.ds(pl.multiple_of(pos * 16, 16), 16)
    for t in range(4):
        tmx[t, mine] = (mix[t, mine].astype(F32) + mrx[t].astype(F32)).astype(BF16)
    spread_mix = Wide(
        lambda yp, h: tmx.at[:, pl.ds(pl.multiple_of(yp * 32 + h * 16, 16), 16)], ws, wr
    )
    spread_mix.send_x()
    tree.wait_a()
    tree.send_b()
    lax.fori_loop(2, 3, weight_up, 0)
    tree.wait_b()
    tree.send_c()
    spread_mix.wait_x()
    spread_mix.send_a()
    lax.fori_loop(3, 4, weight_up, 0)
    for i in range(8):
        for half in range(2):
            dst = ugrad_out.at[i // 4, pl.ds(i % 4 * 256 + half * 128, 128)]
            src = part.at[1, i, c, :, pl.ds(half * 512, 512)]
            cp = pltpu.make_async_copy(src, dst, wgrad_sem.at[8 + i * 2 + half])
            cp.start()
            outs.append(cp)
    total = tree.wait_c()
    bh[0] = total[:, :128].astype(BF16)
    bh[1] = total[:, 128:].astype(BF16)
    cross_back = pltpu.make_async_remote_copy(
        src_ref=bh.at[1 - high],
        dst_ref=bx,
        send_sem=xs.at[1],
        recv_sem=xr.at[1],
        device_id=(dp, (1 - high) * 4 + y),
        device_id_type=MESH,
    )
    cross_back.start()
    spread_mix.wait_a()
    spread_mix.send_b()
    gate_back = dot(lall[:, own].astype(BF16), gate_w[:, own_cols], TN)
    cross_back.wait_recv()
    upstream = bh[high].astype(F32) + bx[...].astype(F32) + gate_back
    gx[pos] = upstream.astype(BF16)
    dall[own] = (upstream * feat[own, own_cols].astype(F32)).astype(BF16)
    scaled = Push("dp", lambda i: dall.at[pl.ds(pl.multiple_of(i * 128, 128), 128)], ds, dr)
    scaled.send()
    spread_g = Wide(lambda yp, h: gx.at[yp * 2 + h], hs, hr)
    spread_g.send_x()
    logits.wait()
    gts[...] = dot(lall[...].astype(BF16), shared[...], NN)
    ost[...] = jnp.sum(lall[...], axis=1, keepdims=True)
    for i, (src, dst) in enumerate(((gts, gating_out), (ost, offset_out))):
        cp = pltpu.make_async_copy(src, dst, out_sem.at[i])
        cp.start()
        outs.append(cp)
    spread_g.wait_x()
    spread_g.send_a()
    scaled.wait()
    half = pl.ds(pl.multiple_of(c * 512, 512), 512)
    crs[pos, c] = dot(dall[...], feat[:, half], TN).T.astype(BF16)
    bias_row = jnp.sum(dall[...].astype(F32), axis=0, keepdims=True)
    biases[pos] = jnp.broadcast_to(bias_row, (8, 128))
    spread_c = Wide(lambda yp, h: crs.at[yp * 2 + h, c], vs, vr)
    spread_c.send_x()

    shares = []

    def share(slot, k):
        cp = pltpu.make_async_remote_copy(
            src_ref=crs.at[slot, c],
            dst_ref=crs.at[slot, c],
            send_sem=ks.at[k],
            recv_sem=kr.at[k],
            device_id=partner,
            device_id_type=MESH,
        )
        cp.start()
        shares.append(cp)

    def slot(dy, h):
        return lax.rem(y + dy + 4, 4) * 2 + h

    share(slot(0, high), 0)
    spread_b = Push("expert", lambda i: biases.at[lax.rem(i, 4) * 2 + i // 4], zs, zr)
    spread_b.send()
    spread_g.wait_a()
    spread_g.send_b()
    spread_c.wait_x()
    spread_c.send_a()
    share(slot(0, 1 - high), 1)
    spread_g.wait_b()
    for i in range(8):
        cols = pl.ds(i * 128, 128)
        grad = gx[i].astype(F32)
        gf[:, cols] = grad
        dus[:, cols] = (grad * feat_in[:, cols].astype(F32)).astype(BF16)
    for n in range(2):
        cols = pl.ds(n * 512, 512)
        update = dot(feat_in[...], wc[:, cols], NN) + bias_in[:, cols]
        grad = gf[:, cols] + dot(dus[...], wc[cols, :], NT) + gf[:, cols] * update
        fgs[:, cols] = grad.astype(BF16)
    spread_mix.wait_b()
    for i, (src, dst) in enumerate(((fgs, fgrad_out), (tmx, mixed_out))):
        cp = pltpu.make_async_copy(src, dst, out_sem.at[2 + i])
        cp.start()
        outs.append(cp)
    spread_c.wait_a()
    spread_c.send_b()
    for i, (dy, h) in enumerate(((1, 0), (1, 1), (-1, 0), (-1, 1))):
        share(slot(dy, h), 2 + i)
    spread_b.wait()
    for i in range(8):
        bst[:, pl.ds(i * 128, 128)] = biases[i, :1]
    cp = pltpu.make_async_copy(bst, bias_out, out_sem.at[4])
    cp.start()
    outs.append(cp)
    spread_c.wait_b()
    for h in range(2):
        share(slot(2, h), 6 + h)
    writes = []
    order = [(0, high), (0, 1 - high), (1, 0), (1, 1), (-1, 0), (-1, 1), (2, 0), (2, 1)]
    for i, (dy, h) in enumerate(order):
        where = slot(dy, h)
        pltpu.make_async_remote_copy(
            src_ref=crs.at[where, 1 - c],
            dst_ref=crs.at[where, 1 - c],
            send_sem=ks.at[i],
            recv_sem=kr.at[i],
            device_id=partner,
            device_id_type=MESH,
        ).wait_recv()
        if i >= 4:
            writes[i - 4].wait()
        for core in range(2):
            cst[i % 4, pl.ds(core * 512, 512)] = crs[where, core].astype(F32)
        dst = cross_out.at[:, pl.ds(pl.multiple_of(where * 128, 128), 128)]
        cp = pltpu.make_async_copy(cst.at[i % 4], dst, cst_sem.at[i])
        cp.start()
        writes.append(cp)
    outs.extend(writes[4:])
    for item in (first, second, mixer, spread_mix, back, tree, parts, logits, scaled, spread_g):
        item.drain()
    for item in (spread_c, spread_b):
        item.drain()
    swap.wait_send()
    cross_mix.wait_send()
    cross_back.wait_send()
    for cp in shares:
        cp.wait_send()
    for cp in outs:
        cp.wait()


def core(features, own_grad, cross_weight, cross_bias, up_weight, down_weight, *tail):
    rows, width = features.shape
    exp_dev, _, hid = up_weight.shape
    every = 16 * rows
    tasks = tail[0].shape[0]
    anywhere = pl.BlockSpec(memory_space=pl.ANY)
    inside = pl.BlockSpec(memory_space=pltpu.VMEM)
    dma = pltpu.SemaphoreType.DMA

    def pairs(*counts):
        return [dma(n if isinstance(n, tuple) else (n,)) for n in counts for _ in range(2)]

    vmem = pltpu.VMEM
    return pl.pallas_call(
        expert_kernel,
        out_shape=(
            jax.ShapeDtypeStruct((tasks, rows, width), BF16),
            jax.ShapeDtypeStruct((rows, width), BF16),
            jax.ShapeDtypeStruct(up_weight.shape, BF16),
            jax.ShapeDtypeStruct(down_weight.shape, BF16),
            jax.ShapeDtypeStruct((width, width), F32),
            jax.ShapeDtypeStruct((1, width), F32),
            jax.ShapeDtypeStruct((64, width), F32),
            jax.ShapeDtypeStruct((64, 1), F32),
        ),
        in_specs=[inside, inside, anywhere, inside, anywhere, anywhere] + [inside] * 4,
        out_specs=[anywhere] * 8,
        scratch_shapes=[
            vmem((every, width), BF16),
            vmem((every, width), BF16),
            vmem((exp_dev, every, width), BF16),
            vmem((width, width), BF16),
            vmem(up_weight.shape, BF16),
            vmem(down_weight.shape, BF16),
            vmem((exp_dev, every, hid), BF16),
            vmem((exp_dev, every, hid), BF16),
            vmem((exp_dev, 8, 2, rows, width), BF16),
            vmem((exp_dev, 8, rows, width), BF16),
            vmem((exp_dev, rows, width), BF16),
            vmem((exp_dev, 3, rows, width), BF16),
            vmem((exp_dev, 3, rows, width), BF16),
            vmem((exp_dev, rows, width), F32),
            vmem((tasks, rows, width), BF16),
            vmem((2, tasks, 16, width), BF16),
            vmem((2, 2, tasks, 16, width), BF16),
            vmem((tasks, 16, width), BF16),
            vmem((tasks, rows, width), BF16),
            vmem((2, 8, rows, 128), BF16),
            vmem((2, 2, 8, rows, 128), BF16),
            vmem((8, rows, 256), BF16),
            vmem((rows, 256), BF16),
            vmem((3, rows, 256), BF16),
            vmem((3, rows, 256), BF16),
            vmem((2, rows, 128), BF16),
            vmem((rows, 128), BF16),
            vmem((8, 8, rows), F32),
            vmem((64, every), F32),
            vmem((8, rows, 128), BF16),
            vmem((every, 128), BF16),
            vmem((8, 2, width // 2, 128), BF16),
            vmem((8, 8, 128), F32),
            vmem((4, width, 128), F32),
            vmem((rows, width), F32),
            vmem((rows, width), BF16),
            vmem((rows, width), BF16),
            vmem((64, width), F32),
            vmem((1, width), F32),
            vmem((64, 1), F32),
            dma((5,)), dma((5,)), dma((24,)), dma((8,)),
            *pairs(17, 17, 3, (2, 9)),
            *pairs(6, 7, 6, 9, 2, 7, 15, 7, 15, 7, 8, 7),
            pltpu.SemaphoreType.REGULAR,
        ],
        compiler_params=pltpu.CompilerParams(
            collective_id=0, has_side_effects=True, vmem_limit_bytes=67043328
        ),
        name="step",
    )(features, own_grad, cross_weight, cross_bias, up_weight, down_weight, *tail)


def local(
    features, cross_weight, cross_bias, gate_weight, gate_offset, up_weight, down_weight, task_grad
):
    rows, tasks, width = task_grad.shape
    exp_dev = up_weight.shape[0]
    rank = lax.axis_index("expert")
    slots = lax.axis_size("expert")
    shared = cross(features, cross_weight[0], cross_bias[0])[1]
    gates = gating(shared, gate_weight, gate_offset, tasks)
    gates = gates.reshape(rows, tasks, slots, exp_dev).transpose(2, 3, 1, 0)
    gates = gates.reshape(slots, exp_dev * tasks, rows)
    gates_own = lax.dynamic_index_in_dim(gates, rank, 0, keepdims=False).T
    task_major = task_grad.transpose(1, 0, 2)
    wide = task_major.astype(F32)
    own_grad = jnp.stack(
        [
            sum(gates_own[:, e * tasks + t, None] * wide[t] for t in range(tasks))
            for e in range(exp_dev)
        ]
    ).astype(BF16)
    gate_rows = gate_weight.T.reshape(tasks, slots, exp_dev, width).transpose(1, 2, 0, 3)
    outs = core(
        features, own_grad, cross_weight[0], cross_bias, up_weight, down_weight,
        task_major, gates, gates_own, gate_rows.reshape(-1, width),
    )
    mixed, feature_grad, up_grad, down_grad, cross_grad, bias_grad, gating_t, offset = outs
    gating_grad = gating_t.reshape(slots, exp_dev, tasks, width).transpose(3, 2, 0, 1)
    offset = offset.reshape(slots, exp_dev, tasks).transpose(2, 0, 1)
    return (
        mixed.transpose(1, 0, 2),
        feature_grad,
        up_grad,
        down_grad,
        cross_grad[None],
        bias_grad,
        gating_grad.reshape(width, -1),
        offset.reshape(-1),
    )


def solution(mesh):
    placed = (
        P("dp", None),
        P(),
        P(),
        P(),
        P(),
        P("expert", None, "dp"),
        P("expert", "dp", None),
        P("dp", None, None),
    )
    return jax.shard_map(
        local,
        mesh=mesh,
        in_specs=placed,
        out_specs=(
            P("dp", None, None),
            P("dp", None),
            P("expert", None, "dp"),
            P("expert", "dp", None),
            P(),
            P(),
            P(),
            P(),
        ),
        check_vma=False,
    )
```

```python
import jax
import jax.numpy as jnp
import numpy as np
from jax import lax
from jax.experimental import pallas as pl
from jax.experimental.pallas import tpu as pltpu
from jax.sharding import PartitionSpec as P

F32 = jnp.float32
BF16 = jnp.bfloat16


MESH = pl.DeviceIdType.MESH
THIRDS = ((0, 48), (48, 48), (96, 32))


def place():
    dp, ex = lax.axis_index("dp"), lax.axis_index("expert")
    z, xl, c = dp // 4, lax.rem(dp // 2, 2), lax.rem(dp, 2)

    def rank(dx, dz, core):
        return lax.rem(z + dz + 4, 4) * 4 + (1 - xl if dx else xl) * 2 + core

    return dp, ex, c, rank


class Spread:
    STEPS = (
        ((0, (0, 0)), (1, (0, 0)), (2, (0, 0))),
        ((3, (0, 1)), (4, (0, 1)), (5, (1, 0))),
        ((6, (0, 2)), (7, (1, 1)), (8, (1, -1))),
    )
    GOT = (
        ((0, (1, 0)), (1, (0, 1)), (2, (0, -1))),
        ((3, (1, 1)), (4, (0, 2)), (5, (1, -1))),
        ((6, (1, 2)), (7, (1, 2)), (8, (1, 2))),
    )
    ORDER = ((0, 0), (1, 0), (0, 1), (0, -1), (1, 1), (0, 2), (1, -1), (1, 2))

    def __init__(self, block, own, ssem, rsem):
        self.block, self.own, self.ssem, self.rsem = block, own, ssem, rsem
        self.dp, self.ex, self.c, self.rank = place()
        self.near = (
            self.rank(1, 0, self.c),
            self.rank(0, -1, self.c),
            self.rank(0, 1, self.c),
        )
        self.sent = []

    def copy(self, src, dst, k, to):
        return pltpu.make_async_remote_copy(
            src_ref=src,
            dst_ref=dst,
            send_sem=self.ssem.at[k],
            recv_sem=self.rsem.at[k],
            device_id=(to, self.ex),
            device_id_type=MESH,
        )

    def send(self, step):
        for i, (k, rel) in enumerate(self.STEPS[step]):
            part = THIRDS[i] if step == 2 else (0, 128)
            dst = self.block(self.rank(*rel, self.c), *part)
            src = self.own if step == 0 else dst
            cp = self.copy(src, dst, k, self.near[i])
            cp.start()
            self.sent.append(cp)

    def wait(self, step):
        for i, (k, rel) in enumerate(self.GOT[step]):
            part = THIRDS[i] if step == 2 else (0, 128)
            dst = self.block(self.rank(*rel, self.c), *part)
            self.copy(dst, dst, k, self.near[i]).wait_recv()

    def share(self, lo, hi):
        for j in range(lo, hi):
            dst = self.block(self.rank(*self.ORDER[j], self.c), 0, 128)
            cp = self.copy(self.own if j == 0 else dst, dst, 9 + j, self.rank(0, 0, 1 - self.c))
            cp.start()
            self.sent.append(cp)

    def wait_shared(self, lo=0, hi=8):
        for j in range(lo, hi):
            dst = self.block(self.rank(*self.ORDER[j], 1 - self.c), 0, 128)
            self.copy(dst, dst, 9 + j, self.rank(0, 0, 1 - self.c)).wait_recv()

    def drain(self):
        for cp in self.sent:
            cp.wait_send()


class Gather:
    def __init__(self, block, ra, rb, rc, ssem, rsem):
        self.block, self.ra, self.rb, self.rc = block, ra, rb, rc
        self.ssem, self.rsem = ssem, rsem
        self.dp, self.ex, self.c, self.rank = place()
        self.x = self.rank(1, 0, self.c)
        self.up = self.rank(0, 1, self.c)
        self.down = self.rank(0, -1, self.c)
        self.sent = []

    def ref(self, dx, dz):
        return self.block(self.rank(dx, dz, 0) // 2)

    def copy(self, src, dst, k, to):
        return pltpu.make_async_remote_copy(
            src_ref=src,
            dst_ref=dst,
            send_sem=self.ssem.at[k],
            recv_sem=self.rsem.at[k],
            device_id=(to, self.ex),
            device_id_type=MESH,
        )

    def go(self, src, dst, k, to):
        cp = self.copy(src, dst, k, to)
        cp.start()
        self.sent.append(cp)

    def add(self, ref, got):
        ref[...] = (ref[...].astype(F32) + got[...].astype(F32)).astype(BF16)

    def send_a(self):
        for i, to in enumerate((self.x, self.up, self.down)):
            rows = pl.ds(*THIRDS[i])
            self.go(self.ref(1, 2).at[rows], self.ra.at[rows], i, to)

    def wait_a(self):
        for i, rel in enumerate(((0, 2), (1, 1), (1, -1))):
            rows = pl.ds(*THIRDS[i])
            got = self.ra.at[rows]
            self.copy(got, got, i, self.x).wait_recv()
            self.add(self.ref(*rel).at[rows], got)

    def send_b(self):
        self.go(self.ref(1, 1), self.rb.at[1], 4, self.x)
        self.go(self.ref(0, 2), self.rb.at[0], 3, self.up)
        self.go(self.ref(1, -1), self.rb.at[2], 5, self.down)

    def wait_b(self):
        for i, rel in enumerate(((0, 1), (0, 1), (1, 0))):
            got = self.rb.at[i]
            self.copy(got, got, 3 + i, self.x).wait_recv()
            self.add(self.ref(*rel), got)

    def send_c(self):
        self.go(self.ref(1, 0), self.rc.at[0], 6, self.x)
        self.go(self.ref(0, 1), self.rc.at[1], 7, self.up)
        self.go(self.ref(0, -1), self.rc.at[2], 8, self.down)

    def wait_c(self):
        total = self.ref(0, 0)[...].astype(F32)
        for i in range(3):
            got = self.rc.at[i]
            self.copy(got, got, 6 + i, self.x).wait_recv()
            total = total + got[...].astype(F32)
        return total

    def drain(self):
        for cp in self.sent:
            cp.wait_send()


class Sides:
    def __init__(self, ref, ssem, rsem):
        self.ref, self.ssem, self.rsem = ref, ssem, rsem
        self.dp, ex = lax.axis_index("dp"), lax.axis_index("expert")
        self.y, self.h = lax.rem(ex, 4), ex // 4
        self.other = (1 - self.h) * 4 + self.y
        self.up = self.h * 4 + lax.rem(self.y + 1, 4)
        self.down = self.h * 4 + lax.rem(self.y + 3, 4)
        self.sent = []

    def at(self, dy, h):
        return self.ref(lax.rem(self.y + dy + 4, 4), h)

    def copy(self, src, dst, k, to):
        return pltpu.make_async_remote_copy(
            src_ref=src,
            dst_ref=dst,
            send_sem=self.ssem.at[k],
            recv_sem=self.rsem.at[k],
            device_id=(self.dp, to),
            device_id_type=MESH,
        )

    def go(self, src, dst, k, to):
        cp = self.copy(src, dst, k, to)
        cp.start()
        self.sent.append(cp)

    def got(self, dst, k):
        self.copy(dst, dst, k, self.other).wait_recv()

    def drain(self):
        for cp in self.sent:
            cp.wait_send()


class Wide(Sides):
    def send_x(self):
        self.go(self.at(0, self.h), self.at(0, self.h), 0, self.other)

    def wait_x(self):
        self.got(self.at(0, 1 - self.h), 0)

    def send_a(self):
        for h in range(2):
            self.go(self.at(0, h), self.at(0, h), 1 + h, self.down)
            self.go(self.at(0, h), self.at(0, h), 3 + h, self.up)

    def wait_a(self):
        for h in range(2):
            self.got(self.at(1, h), 1 + h)
            self.got(self.at(-1, h), 3 + h)

    def send_b(self):
        self.go(self.at(1, 0), self.at(1, 0), 5, self.down)
        self.go(self.at(-1, 1), self.at(-1, 1), 6, self.up)

    def wait_b(self):
        for h in range(2):
            self.got(self.at(2, h), 5 + h)


class Narrow(Sides):
    def __init__(self, ref, ra, rb, ssem, rsem):
        super().__init__(ref, ssem, rsem)
        self.ra, self.rb = ra, rb

    def send_a(self):
        self.go(self.at(2, 0), self.ra.at[0], 0, self.up)
        self.go(self.at(2, 1), self.ra.at[1], 1, self.down)

    def wait_a(self):
        for h, dy in enumerate((1, -1)):
            self.got(self.ra.at[h], h)
            ref, got = self.at(dy, h), self.ra.at[h]

            def add(k, carry):
                ref[k] = (ref[k].astype(F32) + got[k].astype(F32)).astype(BF16)
                return carry

            lax.fori_loop(0, got.shape[0], add, 0)

    def send_b(self):
        for h in range(2):
            self.go(self.at(1, h), self.rb.at[0, h], 2 + h, self.up)
            self.go(self.at(-1, h), self.rb.at[1, h], 4 + h, self.down)

    def wait_b(self, put):
        for h in range(2):
            for d in range(2):
                self.got(self.rb.at[d, h], 2 + 2 * d + h)
            ref = self.at(0, h)

            def add(k, carry):
                total = ref[k].astype(F32) + self.rb[0, h, k].astype(F32)
                put(k, h, (total + self.rb[1, h, k].astype(F32)).astype(BF16))
                return carry

            lax.fori_loop(0, ref.shape[0], add, 0)


class Push:
    def __init__(self, axis, slot, ssem, rsem):
        self.slot, self.ssem, self.rsem = slot, ssem, rsem
        self.n, self.me = lax.axis_size(axis), lax.axis_index(axis)
        if axis == "dp":
            other = lax.axis_index("expert")
            self.to = lambda k: (k, other)
        else:
            other = lax.axis_index("dp")
            self.to = lambda k: (other, k)
        self.sent = []

    def copy(self, i, k, to):
        return pltpu.make_async_remote_copy(
            src_ref=self.slot(i),
            dst_ref=self.slot(i),
            send_sem=self.ssem.at[k - 1],
            recv_sem=self.rsem.at[k - 1],
            device_id=self.to(to),
            device_id_type=MESH,
        )

    def send(self):
        for k in range(1, self.n):
            cp = self.copy(self.me, k, lax.rem(self.me + k, self.n))
            cp.start()
            self.sent.append(cp)

    def wait(self):
        for k in range(1, self.n):
            source = lax.rem(self.me + self.n - k, self.n)
            self.copy(source, k, source).wait_recv()

    def drain(self):
        for cp in self.sent:
            cp.wait_send()


def dot(a, b, dims):
    return lax.dot_general(a, b, (dims, ((), ())), preferred_element_type=F32)


NN, NT, TN = ((1,), (0,)), ((1,), (1,)), ((0,), (0,))


class Exchange:
    def __init__(self, block, got, ssem, rsem):
        self.block, self.got, self.ssem, self.rsem = block, got, ssem, rsem
        dp, ex = lax.axis_index("dp"), lax.axis_index("expert")
        self.chip, self.c, self.y, self.h = dp // 2, lax.rem(dp, 2), lax.rem(ex, 4), ex // 4
        self.sent = []

    def place(self, j):
        chip = lax.rem(self.chip + j % 8, 8)
        return chip, (1 - self.h if j >= 8 else self.h)

    def copy(self, j):
        chip, h = self.place(j)
        return pltpu.make_async_remote_copy(
            src_ref=self.block(chip, h),
            dst_ref=self.got.at[j - 1],
            send_sem=self.ssem.at[j - 1],
            recv_sem=self.rsem.at[j - 1],
            device_id=(chip * 2 + self.c, h * 4 + self.y),
            device_id_type=MESH,
        )

    def send(self):
        for j in range(1, 16):
            cp = self.copy(j)
            cp.start()
            self.sent.append(cp)

    def wait(self):
        total = self.block(self.chip, self.h)[...].astype(F32)
        for j in range(1, 16):
            self.copy(j).wait_recv()
            total = total + self.got[j - 1].astype(F32)
        return total

    def drain(self):
        for cp in self.sent:
            cp.wait_send()


def expert_kernel(
    feat_in, wc_in, bias_in, up_in, down_in, tg, gate_w, gate_off, order_in,
    mixed_out, fgrad_out, ugrad_out, dgrad_out, cross_out, bias_out, gating_out, offset_out,
    feat, shared, og, wc, up, down, act, dsl, part, crecv, ra, rb, rc, group,
    mix, mra, mrb, mrx, tmx, bra, brb, bt, got, gp, lall, gx, dall, crs, biases,
    gf, dus, fgs, gts, bst, ost, gates_all, gates_own,
    load_sem, out_sem, wgrad_sem, fs, fr, gs, gr, cs, cr, ts, tr,
    ms, mr, ws, wr, bs, br, us, ur, xs, xr, ps, pr, ls, lr, hs, hr, ds, dr, vs, vr, ks, kr, zs, zr,
    free,
):
    dp, ex, c, rank = place()
    z, xl = dp // 4, lax.rem(dp // 2, 2)
    y, high = lax.rem(ex, 4), ex // 4
    barrier = pltpu.get_barrier_semaphore()
    for k in range(1, 16):
        to = (lax.rem(dp + k, 16), ex)
        pl.semaphore_signal(barrier, inc=1, device_id=to, device_id_type=MESH)
    for k in range(1, 8):
        to = (dp, lax.rem(ex + k, 8))
        pl.semaphore_signal(barrier, inc=1, device_id=to, device_id_type=MESH)
    for k in range(1, 8):
        to = (lax.rem(dp // 2 + k, 8) * 2 + c, (1 - high) * 4 + y)
        pl.semaphore_signal(barrier, inc=1, device_id=to, device_id_type=MESH)
    loads = [
        pltpu.make_async_copy(src, dst, load_sem.at[i])
        for i, (src, dst) in enumerate((
            (feat_in, feat.at[pl.ds(dp * 128, 128)]),
            (wc_in, wc), (up_in, up), (down_in, down),
        ))
    ]
    for cp in loads:
        cp.start()
    pl.semaphore_wait(barrier, 29)
    partner = (rank(0, 0, 1 - c), ex)
    first = Spread(lambda d, r, n: feat.at[pl.ds(d * 128 + r, n)], feat_in, fs, fr)
    second = [
        Spread(
            lambda d, r, n, e=e: og.at[e, pl.ds(d * 128 + r, n)],
            og.at[e, pl.ds(dp * 128, 128)], gs.at[e], gr.at[e],
        )
        for e in range(2)
    ]
    first.send(0)
    first.share(0, 1)
    for cp in loads:
        cp.wait()
    own = pl.ds(pl.multiple_of(dp * 128, 128), 128)
    base = feat_in[...].astype(F32)
    update = dot(feat_in[...], wc[...], NN) + bias_in[...]
    fgs[...] = (base * update + base).astype(BF16)
    expo = jnp.exp(dot(gate_w[...], fgs[...], NT) + gate_off[...])
    for i in range(8):
        gates_all[i] = expo[i * 8 : i * 8 + 8]
    total = gates_all[0]
    for i in range(1, 8):
        total = total + gates_all[i]
    total = total + pltpu.roll(total, 4, 0)
    for i in range(8):
        gates_all[i] = gates_all[i] / total
    gates_own[...] = jnp.zeros((128, 128), F32)
    gates_own[:8] = gates_all[ex]
    gates_own[...] = gates_own[...].T
    for e in range(2):
        total = gates_own[:, e * 4 : e * 4 + 1] * tg[0].astype(F32)
        for t in range(1, 4):
            total = total + gates_own[:, e * 4 + t : e * 4 + t + 1] * tg[t].astype(F32)
        og[e, own] = total.astype(BF16)

    def hidden(i, carry):
        dx = jnp.where((i == 1) | (i == 4) | (i == 6) | (i == 7), 1, 0)
        dz = jnp.where((i == 5) | (i == 7), 2, jnp.where((i == 3) | (i == 6), 3, 0))
        dz = jnp.where((i == 2) | (i == 4), 1, dz)
        chip = lax.rem(z + dz, 4) * 2 + xl + dx - 2 * xl * dx
        rows = pl.ds(pl.multiple_of(chip * 256, 256), 256)
        for n in range(2):
            cols = pl.ds(n * 512, 512)
            base = feat[rows, cols].astype(F32)
            update = dot(feat[rows, :], wc[:, cols], NN) + bias_in[:, cols]
            shared[rows, cols] = (base * update + base).astype(BF16)
        for e in range(2):
            pre = dot(shared[rows, :], up[e], NN)
            sig = jax.nn.sigmoid(pre)
            act[e, rows] = (pre * sig).astype(BF16)
            dsl[e, rows] = (sig * (1.0 + pre * (1.0 - sig))).astype(BF16)
        return carry

    first.wait_shared(0, 1)
    lax.fori_loop(0, 1, hidden, 0)
    first.wait(0)
    first.send(1)
    first.share(1, 4)
    second[0].send(0)
    second[0].share(0, 1)
    first.wait_shared(1, 4)
    lax.fori_loop(1, 4, hidden, 0)
    first.wait(1)
    first.send(2)
    first.share(4, 7)
    second[1].send(0)
    second[1].share(0, 1)
    first.wait_shared(4, 7)
    lax.fori_loop(4, 7, hidden, 0)
    first.wait(2)
    first.share(7, 8)
    second[0].wait(0)
    second[0].send(1)
    second[0].share(1, 4)
    first.wait_shared(7, 8)
    lax.fori_loop(7, 8, hidden, 0)

    outs = []
    swaps = []
    trees = []
    for e in range(2):
        def forward(k, carry):
            rows = pl.ds(pl.multiple_of(k * 256, 256), 256)
            for n in range(2):
                cols = pl.ds(n * 512, 512)
                out = dot(act[e, rows], down[e, :, cols], NN).astype(BF16)
                part[e, k, 0, :, cols] = out[:128]
                part[e, k, 1, :, cols] = out[128:]
            return carry

        lax.fori_loop(0, 8, forward, 0)
        swap = pltpu.make_async_remote_copy(
            src_ref=part.at[e, :, 1 - c],
            dst_ref=crecv.at[e],
            send_sem=cs.at[e],
            recv_sem=cr.at[e],
            device_id=partner,
            device_id_type=MESH,
        )
        swap.start()
        swaps.append(swap)
        blocks = lambda k, e=e: part.at[e, k, c]
        trees.append(Gather(blocks, ra.at[e], rb.at[e], rc.at[e], ts.at[e], tr.at[e]))
        if e == 0:
            second[1].wait(0)
            second[1].send(1)
            second[1].share(1, 4)
    second[0].wait(1)
    second[0].send(2)
    second[0].share(4, 7)
    for e in range(2):
        swaps[e].wait_recv()

        def merge(k, carry):
            part[e, k, c] = (part[e, k, c].astype(F32) + crecv[e, k].astype(F32)).astype(BF16)
            return carry

        lax.fori_loop(0, 8, merge, 0)
        if e == 0:
            pl.semaphore_signal(free, inc=1, device_id=partner, device_id_type=MESH)
            second[1].wait(1)
            second[1].send(2)
            second[1].share(4, 7)
        trees[e].send_a()
    second[0].wait(2)
    second[0].share(7, 8)
    second[0].wait_shared()

    def backward(k, carry):
        rows = pl.ds(pl.multiple_of(k * 256, 256), 256)
        grad = dot(og[0, rows], down[0], NT)
        dsl[0, rows] = (grad * dsl[0, rows].astype(F32)).astype(BF16)
        return carry

    lax.fori_loop(0, 8, backward, 0)
    second[1].wait(2)
    second[1].share(7, 8)
    for e in range(2):
        trees[e].wait_a()
        trees[e].send_b()
        swaps[e].wait_send()
    second[1].wait_shared()
    pl.semaphore_wait(free, 1)

    def to_shared(k, carry):
        rows = pl.ds(pl.multiple_of(k * 256, 256), 256)
        grad = dot(og[1, rows], down[1], NT)
        dsl[1, rows] = (grad * dsl[1, rows].astype(F32)).astype(BF16)
        for n in range(2):
            cols = pl.ds(n * 512, 512)
            grad = dot(dsl[0, rows], up[0, cols], NT) + dot(dsl[1, rows], up[1, cols], NT)
            part[1 - c, k, 1 - c, :, cols] = grad[:128].astype(BF16)
            part[c, k, 1 - c, :, cols] = grad[128:].astype(BF16)
        return carry

    swaps = []
    backs = []
    for i in range(2):
        lax.fori_loop(i * 4, i * 4 + 4, to_shared, 0)
        swap = pltpu.make_async_remote_copy(
            src_ref=part.at[0, pl.ds(i * 4, 4), 1 - c],
            dst_ref=crecv.at[0, pl.ds(i * 4, 4)],
            send_sem=cs.at[2 + i],
            recv_sem=cr.at[2 + i],
            device_id=partner,
            device_id_type=MESH,
        )
        swap.start()
        swaps.append(swap)
    for i in range(2):
        swaps[i].wait_recv()

        def merge_back(k, carry):
            total = part[1, k, 1 - c].astype(F32) + crecv[0, k].astype(F32)
            part[1, k, 1 - c] = total.astype(BF16)
            return carry

        lax.fori_loop(i * 4, i * 4 + 4, merge_back, 0)
        back = Narrow(
            lambda yp, h, i=i: part.at[
                1, pl.ds(i * 4, 4), 1 - c, :, pl.ds(pl.multiple_of(yp * 256 + h * 128, 128), 128)
            ],
            bra.at[i], brb.at[i], bs.at[i], br.at[i],
        )
        back.send_a()
        backs.append(back)
        trees[i].wait_b()
        trees[i].send_c()

    def weight_down(i, carry):
        e, m = i // 2, lax.rem(i, 2)
        cols = pl.ds(pl.multiple_of(m * 256, 256), 256)
        tile = dot(act[e, :, cols], og[e], TN).astype(BF16)
        crecv[1, i * 2] = tile[:128]
        crecv[1, i * 2 + 1] = tile[128:]
        return carry

    def weight_up(m, carry):
        cols = pl.ds(pl.multiple_of(m * 256, 256), 256)
        for e in range(2):
            tile = dot(shared[:, cols], dsl[e], TN).astype(BF16)
            part[1, e * 4 + m, c, :, :512] = tile[:128]
            part[1, e * 4 + m, c, :, 512:] = tile[128:]
        return carry

    for back in backs:
        back.wait_a()
        back.send_b()
    lax.fori_loop(0, 1, weight_down, 0)
    group[0] = trees[0].wait_c()
    group[1] = trees[1].wait_c()
    trees[0].drain()
    trees[1].drain()

    pos = y * 2 + high
    own_cols = pl.ds(pl.multiple_of(pos * 128, 128), 128)
    lane = lax.broadcasted_iota(jnp.int32, (128, 128), 1)
    packed = jnp.zeros((128, 128), F32)
    for e in range(2):
        for t in range(4):
            inner = jnp.sum(tg[t].astype(F32) * group[e], axis=1, keepdims=True)
            packed = packed + jnp.where(lane == e * 4 + t, inner, 0.0)
    gp[ex] = packed.T[:8]
    parts = Push("expert", lambda i: gp.at[i], ps, pr)
    parts.send()
    for t in range(4):
        mix[t] = (
            gates_own[:, t : t + 1] * group[0] + gates_own[:, t + 4 : t + 5] * group[1]
        ).astype(BF16)
    mixer = Narrow(
        lambda yp, h: mix.at[:, pl.ds(pl.multiple_of(yp * 32 + h * 16, 16), 16)], mra, mrb, ms, mr
    )
    mixer.send_a()

    for i in range(2):
        def keep_back(k, h, total):
            bt[h, i * 4 + k] = total

        backs[i].wait_b(keep_back)
    exchange = Exchange(lambda k, h: bt.at[h, k], got, us, ur)
    exchange.send()
    mixer.wait_a()
    mixer.send_b()
    parts.wait()
    weighed = [gates_all[i] * gp[i] for i in range(8)]
    total = sum(weighed[1:], weighed[0])
    total = total + pltpu.roll(total, 4, 0)
    for i in range(8):
        lall[pl.ds(i * 8, 8), own] = gates_all[i] * (gp[i] - total)
    logits = Push("dp", lambda i: lall.at[:, pl.ds(pl.multiple_of(i * 128, 128), 128)], ls, lr)
    logits.send()
    gate_back = dot(lall[:, own].astype(BF16), gate_w[:, own_cols], TN)
    lax.fori_loop(1, 2, weight_down, 0)
    upstream = exchange.wait() + gate_back
    gx[ex] = upstream.astype(BF16)
    dall[own] = (upstream * feat[own, own_cols].astype(F32)).astype(BF16)
    scaled = Push("dp", lambda i: dall.at[pl.ds(pl.multiple_of(i * 128, 128), 128)], ds, dr)
    scaled.send()
    spread_g = Push("expert", lambda i: gx.at[i], hs, hr)
    spread_g.send()

    def keep_mix(k, h, total):
        mix[k, pl.ds(pl.multiple_of(y * 32 + h * 16, 16), 16)] = total

    mixer.wait_b(keep_mix)
    cross_mix = pltpu.make_async_remote_copy(
        src_ref=mixer.at(0, 1 - high),
        dst_ref=mrx,
        send_sem=xs.at[0],
        recv_sem=xr.at[0],
        device_id=(dp, (1 - high) * 4 + y),
        device_id_type=MESH,
    )
    cross_mix.start()
    lax.fori_loop(2, 3, weight_down, 0)
    cross_mix.wait_recv()
    mine = pl.ds(pl.multiple_of(pos * 16, 16), 16)
    for t in range(4):
        tmx[t, mine] = (mix[t, mine].astype(F32) + mrx[t].astype(F32)).astype(BF16)
    spread_mix = Wide(
        lambda yp, h: tmx.at[:, pl.ds(pl.multiple_of(yp * 32 + h * 16, 16), 16)], ws, wr
    )
    spread_mix.send_x()
    scaled.wait()
    half = pl.ds(pl.multiple_of(c * 512, 512), 512)
    crs[pos, c] = dot(dall[...], feat[:, half], TN).T.astype(BF16)
    spread_c = Push("expert", lambda i: crs.at[lax.rem(i, 4) * 2 + i // 4, c], vs, vr)
    spread_c.send()
    bias_row = jnp.sum(dall[...].astype(F32), axis=0, keepdims=True)
    biases[ex] = jnp.broadcast_to(bias_row, (8, 128))
    spread_b = Push("expert", lambda i: biases.at[i], zs, zr)
    spread_b.send()

    shares = []

    def share(i, k):
        where = lax.rem(i, 4) * 2 + i // 4
        cp = pltpu.make_async_remote_copy(
            src_ref=crs.at[where, c],
            dst_ref=crs.at[where, c],
            send_sem=ks.at[k],
            recv_sem=kr.at[k],
            device_id=partner,
            device_id_type=MESH,
        )
        cp.start()
        shares.append(cp)

    share(ex, 0)
    lax.fori_loop(3, 4, weight_down, 0)
    for i in range(8):
        dst = dgrad_out.at[i // 4, pl.ds(i % 4 * 128, 128)]
        cp = pltpu.make_async_copy(crecv.at[1, i], dst, wgrad_sem.at[i])
        cp.start()
        outs.append(cp)
    spread_mix.wait_x()
    spread_mix.send_a()
    lax.fori_loop(0, 2, weight_up, 0)
    spread_g.wait()
    for i in range(8):
        where = (i % 4) * 2 + i // 4
        cols = pl.ds(where * 128, 128)
        grad = gx[i].astype(F32)
        gf[:, cols] = grad
        dus[:, cols] = (grad * feat_in[:, cols].astype(F32)).astype(BF16)
    for n in range(2):
        cols = pl.ds(n * 512, 512)
        update = dot(feat_in[...], wc[:, cols], NN) + bias_in[:, cols]
        grad = gf[:, cols] + dot(dus[...], wc[cols, :], NT) + gf[:, cols] * update
        fgs[:, cols] = grad.astype(BF16)
    spread_mix.wait_a()
    spread_mix.send_b()
    lax.fori_loop(2, 4, weight_up, 0)
    for i in range(8):
        for part_half in range(2):
            dst = ugrad_out.at[i // 4, pl.ds(i % 4 * 256 + part_half * 128, 128)]
            src = part.at[1, i, c, :, pl.ds(part_half * 512, 512)]
            cp = pltpu.make_async_copy(src, dst, wgrad_sem.at[8 + i * 2 + part_half])
            cp.start()
            outs.append(cp)
    logits.wait()
    ordered = dot(order_in[...].astype(BF16), lall[...].astype(BF16), NN).astype(BF16)
    gts[...] = dot(ordered, shared[...], NN).T
    sums = jnp.broadcast_to(jnp.sum(lall[...], axis=1, keepdims=True), (64, 128))
    sums = lax.dot_general(
        order_in[...], sums, (NN, ((), ())),
        precision=lax.Precision.HIGHEST, preferred_element_type=F32,
    )
    ost[...] = sums.T[:1]
    for i, (src, dst) in enumerate(((gts, gating_out), (ost, offset_out), (fgs, fgrad_out))):
        cp = pltpu.make_async_copy(src, dst, out_sem.at[i])
        cp.start()
        outs.append(cp)
    def write(source, core, k):
        where = lax.rem(source, 4) * 2 + source // 4
        dst = cross_out.at[
            pl.ds(pl.multiple_of(core * 512, 512), 512),
            pl.ds(pl.multiple_of(where * 128, 128), 128),
        ]
        cp = pltpu.make_async_copy(crs.at[where, core], dst, wgrad_sem.at[24 + k])
        cp.start()
        outs.append(cp)

    write(ex, c, 0)
    for k in range(1, 8):
        source = lax.rem(ex + 8 - k, 8)
        spread_c.copy(source, k, source).wait_recv()
        share(source, k)
        write(source, c, k)
    spread_mix.wait_b()
    cp = pltpu.make_async_copy(tmx, mixed_out, out_sem.at[3])
    cp.start()
    outs.append(cp)
    spread_b.wait()
    for i in range(8):
        where = (i % 4) * 2 + i // 4
        bst[:, pl.ds(where * 128, 128)] = biases[i, :1]
    cp = pltpu.make_async_copy(bst, bias_out, out_sem.at[4])
    cp.start()
    outs.append(cp)
    for k in range(8):
        source = lax.rem(ex + 8 - k, 8)
        where = lax.rem(source, 4) * 2 + source // 4
        pltpu.make_async_remote_copy(
            src_ref=crs.at[where, 1 - c],
            dst_ref=crs.at[where, 1 - c],
            send_sem=ks.at[k],
            recv_sem=kr.at[k],
            device_id=partner,
            device_id_type=MESH,
        ).wait_recv()
        write(source, 1 - c, 8 + k)
    for item in (first, *second, mixer, spread_mix, *backs, exchange, parts, logits, scaled):
        item.drain()
    for item in (spread_g, spread_c, spread_b):
        item.drain()
    for swap in swaps:
        swap.wait_send()
    cross_mix.wait_send()
    for cp in shares:
        cp.wait_send()
    for cp in outs:
        cp.wait()


def core(features, cross_weight, cross_bias, up_weight, down_weight, *tail):
    rows, width = features.shape
    exp_dev, _, hid = up_weight.shape
    every = 16 * rows
    tasks = tail[0].shape[0]
    anywhere = pl.BlockSpec(memory_space=pl.ANY)
    inside = pl.BlockSpec(memory_space=pltpu.VMEM)
    dma = pltpu.SemaphoreType.DMA

    def pairs(*counts):
        return [dma(n if isinstance(n, tuple) else (n,)) for n in counts for _ in range(2)]

    vmem = pltpu.VMEM
    return pl.pallas_call(
        expert_kernel,
        out_shape=(
            jax.ShapeDtypeStruct((tasks, rows, width), BF16),
            jax.ShapeDtypeStruct((rows, width), BF16),
            jax.ShapeDtypeStruct(up_weight.shape, BF16),
            jax.ShapeDtypeStruct(down_weight.shape, BF16),
            jax.ShapeDtypeStruct((width, width), BF16),
            jax.ShapeDtypeStruct((1, width), F32),
            jax.ShapeDtypeStruct((width, 64), F32),
            jax.ShapeDtypeStruct((1, 64), F32),
        ),
        in_specs=[inside, anywhere, inside, anywhere, anywhere] + [inside] * 4,
        out_specs=[anywhere] * 8,
        scratch_shapes=[
            vmem((every, width), BF16),
            vmem((every, width), BF16),
            vmem((exp_dev, every, width), BF16),
            vmem((width, width), BF16),
            vmem(up_weight.shape, BF16),
            vmem(down_weight.shape, BF16),
            vmem((exp_dev, every, hid), BF16),
            vmem((exp_dev, every, hid), BF16),
            vmem((exp_dev, 8, 2, rows, width), BF16),
            vmem((exp_dev, 8, rows, width), BF16),
            vmem((exp_dev, rows, width), BF16),
            vmem((exp_dev, 3, rows, width), BF16),
            vmem((exp_dev, 3, rows, width), BF16),
            vmem((exp_dev, rows, width), F32),
            vmem((tasks, rows, width), BF16),
            vmem((2, tasks, 16, width), BF16),
            vmem((2, 2, tasks, 16, width), BF16),
            vmem((tasks, 16, width), BF16),
            vmem((tasks, rows, width), BF16),
            vmem((2, 2, 4, rows, 128), BF16),
            vmem((2, 2, 2, 4, rows, 128), BF16),
            vmem((2, 8, rows, 128), BF16),
            vmem((15, rows, 128), BF16),
            vmem((8, 8, rows), F32),
            vmem((64, every), F32),
            vmem((8, rows, 128), BF16),
            vmem((every, 128), BF16),
            vmem((8, 2, width // 2, 128), BF16),
            vmem((8, 8, 128), F32),
            vmem((rows, width), F32),
            vmem((rows, width), BF16),
            vmem((rows, width), BF16),
            vmem((width, 64), F32),
            vmem((1, width), F32),
            vmem((1, 64), F32),
            vmem((8, 8, rows), F32),
            vmem((rows, 128), F32),
            dma((4,)), dma((5,)), dma((40,)),
            *pairs(17, (2, 17), 4, (2, 9)),
            *pairs(6, 7, (2, 6), 15, 1, 7, 15, 7, 15, 7, 8, 7),
            pltpu.SemaphoreType.REGULAR,
        ],
        compiler_params=pltpu.CompilerParams(
            collective_id=0, has_side_effects=True, vmem_limit_bytes=67043328
        ),
        name="step",
    )(features, cross_weight, cross_bias, up_weight, down_weight, *tail)


def local(
    features, cross_weight, cross_bias, gate_weight, gate_offset, up_weight, down_weight, task_grad
):
    width = features.shape[1]
    tasks = task_grad.shape[1]
    exp_dev = up_weight.shape[0]
    slots = lax.axis_size("expert")
    gates = tasks * slots * exp_dev
    columns = np.arange(gates).reshape(tasks, slots, exp_dev).transpose(1, 2, 0).reshape(-1)
    order = np.zeros((gates, gates), np.float32)
    order[columns, np.arange(gates)] = 1.0
    gate_rows = gate_weight.T.reshape(tasks, slots, exp_dev, width).transpose(1, 2, 0, 3)
    offsets = gate_offset.reshape(tasks, slots, exp_dev).transpose(1, 2, 0).reshape(-1, 1)
    outs = core(
        features, cross_weight[0], cross_bias, up_weight, down_weight,
        task_grad.transpose(1, 0, 2), gate_rows.reshape(-1, width), offsets, jnp.asarray(order),
    )
    mixed, feature_grad, up_grad, down_grad, cross_grad, bias_grad, gating_grad, offset = outs
    return (
        mixed.transpose(1, 0, 2),
        feature_grad,
        up_grad,
        down_grad,
        cross_grad[None].astype(F32),
        bias_grad,
        gating_grad,
        offset.reshape(-1),
    )


def solution(mesh):
    placed = (
        P("dp", None),
        P(),
        P(),
        P(),
        P(),
        P("expert", None, "dp"),
        P("expert", "dp", None),
        P("dp", None, None),
    )
    return jax.shard_map(
        local,
        mesh=mesh,
        in_specs=placed,
        out_specs=(
            P("dp", None, None),
            P("dp", None),
            P("expert", None, "dp"),
            P("expert", "dp", None),
            P(),
            P(),
            P(),
            P(),
        ),
        check_vma=False,
    )
```

```python
import jax
import jax.numpy as jnp
import numpy as np
from jax import lax
from jax.experimental import pallas as pl
from jax.experimental.pallas import tpu as pltpu
from jax.sharding import PartitionSpec as P

F32 = jnp.float32
BF16 = jnp.bfloat16


MESH = pl.DeviceIdType.MESH
THIRDS = ((0, 48), (48, 48), (96, 32))


def place():
    dp, ex = lax.axis_index("dp"), lax.axis_index("expert")
    z, xl, c = dp // 4, lax.rem(dp // 2, 2), lax.rem(dp, 2)

    def rank(dx, dz, core):
        return lax.rem(z + dz + 4, 4) * 4 + (1 - xl if dx else xl) * 2 + core

    return dp, ex, c, rank


class Spread:
    STEPS = (
        ((0, (0, 0)), (1, (0, 0)), (2, (0, 0))),
        ((3, (0, 1)), (4, (0, 1)), (5, (1, 0))),
        ((6, (0, 2)), (7, (1, 1)), (8, (1, -1))),
    )
    GOT = (
        ((0, (1, 0)), (1, (0, 1)), (2, (0, -1))),
        ((3, (1, 1)), (4, (0, 2)), (5, (1, -1))),
        ((6, (1, 2)), (7, (1, 2)), (8, (1, 2))),
    )
    ORDER = ((0, 0), (1, 0), (0, 1), (0, -1), (1, 1), (0, 2), (1, -1), (1, 2))

    def __init__(self, block, own, ssem, rsem):
        self.block, self.own, self.ssem, self.rsem = block, own, ssem, rsem
        self.dp, self.ex, self.c, self.rank = place()
        self.near = (
            self.rank(1, 0, self.c),
            self.rank(0, -1, self.c),
            self.rank(0, 1, self.c),
        )
        self.sent = []

    def copy(self, src, dst, k, to):
        return pltpu.make_async_remote_copy(
            src_ref=src,
            dst_ref=dst,
            send_sem=self.ssem.at[k],
            recv_sem=self.rsem.at[k],
            device_id=(to, self.ex),
            device_id_type=MESH,
        )

    def send(self, step):
        for i, (k, rel) in enumerate(self.STEPS[step]):
            part = THIRDS[i] if step == 2 else (0, 128)
            dst = self.block(self.rank(*rel, self.c), *part)
            src = self.own if step == 0 else dst
            cp = self.copy(src, dst, k, self.near[i])
            cp.start()
            self.sent.append(cp)

    def wait(self, step):
        for i, (k, rel) in enumerate(self.GOT[step]):
            part = THIRDS[i] if step == 2 else (0, 128)
            dst = self.block(self.rank(*rel, self.c), *part)
            self.copy(dst, dst, k, self.near[i]).wait_recv()

    def share(self, lo, hi):
        for j in range(lo, hi):
            dst = self.block(self.rank(*self.ORDER[j], self.c), 0, 128)
            cp = self.copy(self.own if j == 0 else dst, dst, 9 + j, self.rank(0, 0, 1 - self.c))
            cp.start()
            self.sent.append(cp)

    def wait_shared(self, lo=0, hi=8):
        for j in range(lo, hi):
            dst = self.block(self.rank(*self.ORDER[j], 1 - self.c), 0, 128)
            self.copy(dst, dst, 9 + j, self.rank(0, 0, 1 - self.c)).wait_recv()

    def drain(self):
        for cp in self.sent:
            cp.wait_send()


class Gather:
    def __init__(self, block, ra, rb, rc, ssem, rsem):
        self.block, self.ra, self.rb, self.rc = block, ra, rb, rc
        self.ssem, self.rsem = ssem, rsem
        self.dp, self.ex, self.c, self.rank = place()
        self.x = self.rank(1, 0, self.c)
        self.up = self.rank(0, 1, self.c)
        self.down = self.rank(0, -1, self.c)
        self.sent = []

    def ref(self, dx, dz):
        return self.block(self.rank(dx, dz, 0) // 2)

    def copy(self, src, dst, k, to):
        return pltpu.make_async_remote_copy(
            src_ref=src,
            dst_ref=dst,
            send_sem=self.ssem.at[k],
            recv_sem=self.rsem.at[k],
            device_id=(to, self.ex),
            device_id_type=MESH,
        )

    def go(self, src, dst, k, to):
        cp = self.copy(src, dst, k, to)
        cp.start()
        self.sent.append(cp)

    def add(self, ref, got):
        ref[...] = (ref[...].astype(F32) + got[...].astype(F32)).astype(BF16)

    def send_a(self):
        for i, to in enumerate((self.x, self.up, self.down)):
            rows = pl.ds(*THIRDS[i])
            self.go(self.ref(1, 2).at[rows], self.ra.at[rows], i, to)

    def wait_a(self):
        for i, rel in enumerate(((0, 2), (1, 1), (1, -1))):
            rows = pl.ds(*THIRDS[i])
            got = self.ra.at[rows]
            self.copy(got, got, i, self.x).wait_recv()
            self.add(self.ref(*rel).at[rows], got)

    def send_b(self):
        self.go(self.ref(1, 1), self.rb.at[1], 4, self.x)
        self.go(self.ref(0, 2), self.rb.at[0], 3, self.up)
        self.go(self.ref(1, -1), self.rb.at[2], 5, self.down)

    def wait_b(self):
        for i, rel in enumerate(((0, 1), (0, 1), (1, 0))):
            got = self.rb.at[i]
            self.copy(got, got, 3 + i, self.x).wait_recv()
            self.add(self.ref(*rel), got)

    def send_c(self):
        self.go(self.ref(1, 0), self.rc.at[0], 6, self.x)
        self.go(self.ref(0, 1), self.rc.at[1], 7, self.up)
        self.go(self.ref(0, -1), self.rc.at[2], 8, self.down)

    def wait_c(self):
        total = self.ref(0, 0)[...].astype(F32)
        for i in range(3):
            got = self.rc.at[i]
            self.copy(got, got, 6 + i, self.x).wait_recv()
            total = total + got[...].astype(F32)
        return total

    def drain(self):
        for cp in self.sent:
            cp.wait_send()


class Sides:
    def __init__(self, ref, ssem, rsem):
        self.ref, self.ssem, self.rsem = ref, ssem, rsem
        self.dp, ex = lax.axis_index("dp"), lax.axis_index("expert")
        self.y, self.h = lax.rem(ex, 4), ex // 4
        self.other = (1 - self.h) * 4 + self.y
        self.up = self.h * 4 + lax.rem(self.y + 1, 4)
        self.down = self.h * 4 + lax.rem(self.y + 3, 4)
        self.sent = []

    def at(self, dy, h):
        return self.ref(lax.rem(self.y + dy + 4, 4), h)

    def copy(self, src, dst, k, to):
        return pltpu.make_async_remote_copy(
            src_ref=src,
            dst_ref=dst,
            send_sem=self.ssem.at[k],
            recv_sem=self.rsem.at[k],
            device_id=(self.dp, to),
            device_id_type=MESH,
        )

    def go(self, src, dst, k, to):
        cp = self.copy(src, dst, k, to)
        cp.start()
        self.sent.append(cp)

    def got(self, dst, k):
        self.copy(dst, dst, k, self.other).wait_recv()

    def drain(self):
        for cp in self.sent:
            cp.wait_send()


class Wide(Sides):
    def send_x(self):
        self.go(self.at(0, self.h), self.at(0, self.h), 0, self.other)

    def wait_x(self):
        self.got(self.at(0, 1 - self.h), 0)

    def send_a(self):
        for h in range(2):
            self.go(self.at(0, h), self.at(0, h), 1 + h, self.down)
            self.go(self.at(0, h), self.at(0, h), 3 + h, self.up)

    def wait_a(self):
        for h in range(2):
            self.got(self.at(1, h), 1 + h)
            self.got(self.at(-1, h), 3 + h)

    def send_b(self):
        self.go(self.at(1, 0), self.at(1, 0), 5, self.down)
        self.go(self.at(-1, 1), self.at(-1, 1), 6, self.up)

    def wait_b(self):
        for h in range(2):
            self.got(self.at(2, h), 5 + h)


class Narrow(Sides):
    def __init__(self, ref, ra, rb, ssem, rsem):
        super().__init__(ref, ssem, rsem)
        self.ra, self.rb = ra, rb

    def send_a(self):
        self.go(self.at(2, 0), self.ra.at[0], 0, self.up)
        self.go(self.at(2, 1), self.ra.at[1], 1, self.down)

    def wait_a(self):
        for h, dy in enumerate((1, -1)):
            self.got(self.ra.at[h], h)
            ref, got = self.at(dy, h), self.ra.at[h]

            def add(k, carry):
                ref[k] = (ref[k].astype(F32) + got[k].astype(F32)).astype(BF16)
                return carry

            lax.fori_loop(0, got.shape[0], add, 0)

    def send_b(self):
        for h in range(2):
            self.go(self.at(1, h), self.rb.at[0, h], 2 + h, self.up)
            self.go(self.at(-1, h), self.rb.at[1, h], 4 + h, self.down)

    def wait_b(self, put):
        for h in range(2):
            for d in range(2):
                self.got(self.rb.at[d, h], 2 + 2 * d + h)
            ref = self.at(0, h)

            def add(k, carry):
                total = ref[k].astype(F32) + self.rb[0, h, k].astype(F32)
                put(k, h, (total + self.rb[1, h, k].astype(F32)).astype(BF16))
                return carry

            lax.fori_loop(0, ref.shape[0], add, 0)


class Push:
    def __init__(self, axis, slot, ssem, rsem):
        self.slot, self.ssem, self.rsem = slot, ssem, rsem
        self.n, self.me = lax.axis_size(axis), lax.axis_index(axis)
        if axis == "dp":
            other = lax.axis_index("expert")
            self.to = lambda k: (k, other)
        else:
            other = lax.axis_index("dp")
            self.to = lambda k: (other, k)
        self.sent = []

    def copy(self, i, k, to):
        return pltpu.make_async_remote_copy(
            src_ref=self.slot(i),
            dst_ref=self.slot(i),
            send_sem=self.ssem.at[k - 1],
            recv_sem=self.rsem.at[k - 1],
            device_id=self.to(to),
            device_id_type=MESH,
        )

    def send(self):
        for k in range(1, self.n):
            cp = self.copy(self.me, k, lax.rem(self.me + k, self.n))
            cp.start()
            self.sent.append(cp)

    def wait(self):
        for k in range(1, self.n):
            source = lax.rem(self.me + self.n - k, self.n)
            self.copy(source, k, source).wait_recv()

    def drain(self):
        for cp in self.sent:
            cp.wait_send()


def dot(a, b, dims):
    return lax.dot_general(a, b, (dims, ((), ())), preferred_element_type=F32)


NN, NT, TN = ((1,), (0,)), ((1,), (1,)), ((0,), (0,))


class Exchange:
    def __init__(self, block, got, ssem, rsem):
        self.block, self.got, self.ssem, self.rsem = block, got, ssem, rsem
        dp, ex = lax.axis_index("dp"), lax.axis_index("expert")
        self.chip, self.c, self.y, self.h = dp // 2, lax.rem(dp, 2), lax.rem(ex, 4), ex // 4
        self.sent = []

    def place(self, j):
        chip = lax.rem(self.chip + j % 8, 8)
        return chip, (1 - self.h if j >= 8 else self.h)

    def copy(self, j):
        chip, h = self.place(j)
        return pltpu.make_async_remote_copy(
            src_ref=self.block(chip, h),
            dst_ref=self.got.at[j - 1],
            send_sem=self.ssem.at[j - 1],
            recv_sem=self.rsem.at[j - 1],
            device_id=(chip * 2 + self.c, h * 4 + self.y),
            device_id_type=MESH,
        )

    def send(self):
        for j in range(1, 16):
            cp = self.copy(j)
            cp.start()
            self.sent.append(cp)

    def wait(self):
        total = self.block(self.chip, self.h)[...].astype(F32)
        for j in range(1, 16):
            self.copy(j).wait_recv()
            total = total + self.got[j - 1].astype(F32)
        return total

    def drain(self):
        for cp in self.sent:
            cp.wait_send()


def expert_kernel(
    feat_in, wc_in, bias_in, up_in, down_in, tg_in, gate_in, gate_off, order_in,
    mixed_out, fgrad_out, ugrad_out, dgrad_out, cross_out, bias_out, gating_out, offset_out,
    feat, shared, og, wc, up, down, act, dsl, part, crecv, ra, rb, rc, group,
    mix, mra, mrb, mrx, tmx, bra, brb, bt, got, gp, lall, gx, dall, crs, biases,
    gf, dus, fgs, gts, bst, ost, gates_all, gates_own, tg, gate_w,
    load_sem, out_sem, wgrad_sem, fs, fr, gs, gr, cs, cr, ts, tr,
    ms, mr, ws, wr, bs, br, us, ur, xs, xr, ps, pr, ls, lr, hs, hr, ds, dr, vs, vr, ks, kr, zs, zr,
    free,
):
    dp, ex, c, rank = place()
    z, xl = dp // 4, lax.rem(dp // 2, 2)
    y, high = lax.rem(ex, 4), ex // 4
    barrier = pltpu.get_barrier_semaphore()
    for k in range(1, 16):
        to = (lax.rem(dp + k, 16), ex)
        pl.semaphore_signal(barrier, inc=1, device_id=to, device_id_type=MESH)
    for k in range(1, 8):
        to = (dp, lax.rem(ex + k, 8))
        pl.semaphore_signal(barrier, inc=1, device_id=to, device_id_type=MESH)
    for k in range(1, 8):
        to = (lax.rem(dp // 2 + k, 8) * 2 + c, (1 - high) * 4 + y)
        pl.semaphore_signal(barrier, inc=1, device_id=to, device_id_type=MESH)
    loads = [
        pltpu.make_async_copy(src, dst, load_sem.at[i])
        for i, (src, dst) in enumerate((
            (feat_in, feat.at[pl.ds(dp * 128, 128)]),
            (wc_in, wc), (up_in, up), (down_in, down),
        ))
    ]
    for cp in loads:
        cp.start()
    pl.semaphore_wait(barrier, 29)
    partner = (rank(0, 0, 1 - c), ex)
    first = Spread(lambda d, r, n: feat.at[pl.ds(d * 128 + r, n)], feat_in, fs, fr)
    second = [
        Spread(
            lambda d, r, n, e=e: og.at[e, pl.ds(d * 128 + r, n)],
            og.at[e, pl.ds(dp * 128, 128)], gs.at[e], gr.at[e],
        )
        for e in range(2)
    ]
    first.send(0)
    first.share(0, 1)
    for cp in loads:
        cp.wait()
    for t in range(4):
        tg[t] = tg_in[:, t, :]
    own = pl.ds(pl.multiple_of(dp * 128, 128), 128)
    base = feat_in[...].astype(F32)
    update = dot(feat_in[...], wc[...], NN) + bias_in[...]
    fgs[...] = (base * update + base).astype(BF16)
    gate_w[...] = dot(order_in[...].astype(BF16), gate_in[...], TN).astype(BF16)
    offsets = lax.dot_general(
        order_in[...], jnp.broadcast_to(gate_off[...], (128, 64)), (((0,), (1,)), ((), ())),
        precision=lax.Precision.HIGHEST, preferred_element_type=F32,
    )
    expo = jnp.exp(dot(gate_w[...], fgs[...], NT) + offsets)
    for i in range(8):
        gates_all[i] = expo[i * 8 : i * 8 + 8]
    total = gates_all[0]
    for i in range(1, 8):
        total = total + gates_all[i]
    total = total + pltpu.roll(total, 4, 0)
    for i in range(8):
        gates_all[i] = gates_all[i] / total
    gates_own[...] = jnp.zeros((128, 128), F32)
    gates_own[:8] = gates_all[ex]
    gates_own[...] = gates_own[...].T
    for e in range(2):
        total = gates_own[:, e * 4 : e * 4 + 1] * tg[0].astype(F32)
        for t in range(1, 4):
            total = total + gates_own[:, e * 4 + t : e * 4 + t + 1] * tg[t].astype(F32)
        og[e, own] = total.astype(BF16)

    def hidden(i, carry):
        dx = jnp.where((i == 1) | (i == 4) | (i == 6) | (i == 7), 1, 0)
        dz = jnp.where((i == 5) | (i == 7), 2, jnp.where((i == 3) | (i == 6), 3, 0))
        dz = jnp.where((i == 2) | (i == 4), 1, dz)
        chip = lax.rem(z + dz, 4) * 2 + xl + dx - 2 * xl * dx
        rows = pl.ds(pl.multiple_of(chip * 256, 256), 256)
        for n in range(2):
            cols = pl.ds(n * 512, 512)
            base = feat[rows, cols].astype(F32)
            update = dot(feat[rows, :], wc[:, cols], NN) + bias_in[:, cols]
            shared[rows, cols] = (base * update + base).astype(BF16)
        for e in range(2):
            pre = dot(shared[rows, :], up[e], NN)
            sig = jax.nn.sigmoid(pre)
            act[e, rows] = (pre * sig).astype(BF16)
            dsl[e, rows] = (sig * (1.0 + pre * (1.0 - sig))).astype(BF16)
        return carry

    first.wait_shared(0, 1)
    lax.fori_loop(0, 1, hidden, 0)
    first.wait(0)
    first.send(1)
    first.share(1, 4)
    second[0].send(0)
    second[0].share(0, 1)
    first.wait_shared(1, 4)
    lax.fori_loop(1, 4, hidden, 0)
    first.wait(1)
    first.send(2)
    first.share(4, 7)
    second[1].send(0)
    second[1].share(0, 1)
    first.wait_shared(4, 7)
    lax.fori_loop(4, 7, hidden, 0)
    first.wait(2)
    first.share(7, 8)
    second[0].wait(0)
    second[0].send(1)
    second[0].share(1, 4)
    first.wait_shared(7, 8)
    lax.fori_loop(7, 8, hidden, 0)

    outs = []
    swaps = []
    trees = []
    for e in range(2):
        def forward(k, carry):
            rows = pl.ds(pl.multiple_of(k * 256, 256), 256)
            for n in range(2):
                cols = pl.ds(n * 512, 512)
                out = dot(act[e, rows], down[e, :, cols], NN).astype(BF16)
                part[e, k, 0, :, cols] = out[:128]
                part[e, k, 1, :, cols] = out[128:]
            return carry

        lax.fori_loop(0, 8, forward, 0)
        swap = pltpu.make_async_remote_copy(
            src_ref=part.at[e, :, 1 - c],
            dst_ref=crecv.at[e],
            send_sem=cs.at[e],
            recv_sem=cr.at[e],
            device_id=partner,
            device_id_type=MESH,
        )
        swap.start()
        swaps.append(swap)
        blocks = lambda k, e=e: part.at[e, k, c]
        trees.append(Gather(blocks, ra.at[e], rb.at[e], rc.at[e], ts.at[e], tr.at[e]))
        if e == 0:
            second[1].wait(0)
            second[1].send(1)
            second[1].share(1, 4)
    second[0].wait(1)
    second[0].send(2)
    second[0].share(4, 7)
    for e in range(2):
        swaps[e].wait_recv()

        def merge(k, carry):
            part[e, k, c] = (part[e, k, c].astype(F32) + crecv[e, k].astype(F32)).astype(BF16)
            return carry

        lax.fori_loop(0, 8, merge, 0)
        if e == 0:
            pl.semaphore_signal(free, inc=1, device_id=partner, device_id_type=MESH)
            second[1].wait(1)
            second[1].send(2)
            second[1].share(4, 7)
        trees[e].send_a()
    second[0].wait(2)
    second[0].share(7, 8)
    second[0].wait_shared()

    def backward(k, carry):
        rows = pl.ds(pl.multiple_of(k * 256, 256), 256)
        grad = dot(og[0, rows], down[0], NT)
        dsl[0, rows] = (grad * dsl[0, rows].astype(F32)).astype(BF16)
        return carry

    lax.fori_loop(0, 8, backward, 0)
    second[1].wait(2)
    second[1].share(7, 8)
    for e in range(2):
        trees[e].wait_a()
        trees[e].send_b()
        swaps[e].wait_send()
    second[1].wait_shared()
    pl.semaphore_wait(free, 1)

    def to_shared(k, carry):
        rows = pl.ds(pl.multiple_of(k * 256, 256), 256)
        grad = dot(og[1, rows], down[1], NT)
        dsl[1, rows] = (grad * dsl[1, rows].astype(F32)).astype(BF16)
        for n in range(2):
            cols = pl.ds(n * 512, 512)
            grad = dot(dsl[0, rows], up[0, cols], NT) + dot(dsl[1, rows], up[1, cols], NT)
            part[1 - c, k, 1 - c, :, cols] = grad[:128].astype(BF16)
            part[c, k, 1 - c, :, cols] = grad[128:].astype(BF16)
        return carry

    swaps = []
    backs = []
    for i in range(2):
        lax.fori_loop(i * 4, i * 4 + 4, to_shared, 0)
        swap = pltpu.make_async_remote_copy(
            src_ref=part.at[0, pl.ds(i * 4, 4), 1 - c],
            dst_ref=crecv.at[0, pl.ds(i * 4, 4)],
            send_sem=cs.at[2 + i],
            recv_sem=cr.at[2 + i],
            device_id=partner,
            device_id_type=MESH,
        )
        swap.start()
        swaps.append(swap)
    for i in range(2):
        swaps[i].wait_recv()

        def merge_back(k, carry):
            total = part[1, k, 1 - c].astype(F32) + crecv[0, k].astype(F32)
            part[1, k, 1 - c] = total.astype(BF16)
            return carry

        lax.fori_loop(i * 4, i * 4 + 4, merge_back, 0)
        back = Narrow(
            lambda yp, h, i=i: part.at[
                1, pl.ds(i * 4, 4), 1 - c, :, pl.ds(pl.multiple_of(yp * 256 + h * 128, 128), 128)
            ],
            bra.at[i], brb.at[i], bs.at[i], br.at[i],
        )
        back.send_a()
        backs.append(back)
        trees[i].wait_b()
        trees[i].send_c()

    def weight_down(i, carry):
        e, m = i // 2, lax.rem(i, 2)
        cols = pl.ds(pl.multiple_of(m * 256, 256), 256)
        tile = dot(act[e, :, cols], og[e], TN).astype(BF16)
        crecv[1, i * 2] = tile[:128]
        crecv[1, i * 2 + 1] = tile[128:]
        return carry

    def weight_up(m, carry):
        cols = pl.ds(pl.multiple_of(m * 256, 256), 256)
        for e in range(2):
            tile = dot(shared[:, cols], dsl[e], TN).astype(BF16)
            part[1, e * 4 + m, c, :, :512] = tile[:128]
            part[1, e * 4 + m, c, :, 512:] = tile[128:]
        return carry

    for back in backs:
        back.wait_a()
        back.send_b()
    lax.fori_loop(0, 1, weight_down, 0)
    group[0] = trees[0].wait_c()
    group[1] = trees[1].wait_c()
    trees[0].drain()
    trees[1].drain()

    pos = y * 2 + high
    own_cols = pl.ds(pl.multiple_of(pos * 128, 128), 128)
    lane = lax.broadcasted_iota(jnp.int32, (128, 128), 1)
    packed = jnp.zeros((128, 128), F32)
    for e in range(2):
        for t in range(4):
            inner = jnp.sum(tg[t].astype(F32) * group[e], axis=1, keepdims=True)
            packed = packed + jnp.where(lane == e * 4 + t, inner, 0.0)
    gp[ex] = packed.T[:8]
    parts = Push("expert", lambda i: gp.at[i], ps, pr)
    parts.send()
    for t in range(4):
        mix[t] = (
            gates_own[:, t : t + 1] * group[0] + gates_own[:, t + 4 : t + 5] * group[1]
        ).astype(BF16)
    mixer = Narrow(
        lambda yp, h: mix.at[:, pl.ds(pl.multiple_of(yp * 32 + h * 16, 16), 16)], mra, mrb, ms, mr
    )
    mixer.send_a()

    for i in range(2):
        def keep_back(k, h, total):
            bt[h, i * 4 + k] = total

        backs[i].wait_b(keep_back)
    exchange = Exchange(lambda k, h: bt.at[h, k], got, us, ur)
    exchange.send()
    mixer.wait_a()
    mixer.send_b()
    parts.wait()
    weighed = [gates_all[i] * gp[i] for i in range(8)]
    total = sum(weighed[1:], weighed[0])
    total = total + pltpu.roll(total, 4, 0)
    for i in range(8):
        lall[pl.ds(i * 8, 8), own] = gates_all[i] * (gp[i] - total)
    logits = Push("dp", lambda i: lall.at[:, pl.ds(pl.multiple_of(i * 128, 128), 128)], ls, lr)
    logits.send()
    gate_back = dot(lall[:, own].astype(BF16), gate_w[:, own_cols], TN)
    lax.fori_loop(1, 2, weight_down, 0)
    def keep_mix(k, h, total):
        mix[k, pl.ds(pl.multiple_of(y * 32 + h * 16, 16), 16)] = total

    mixer.wait_b(keep_mix)
    cross_mix = pltpu.make_async_remote_copy(
        src_ref=mixer.at(0, 1 - high),
        dst_ref=mrx,
        send_sem=xs.at[0],
        recv_sem=xr.at[0],
        device_id=(dp, (1 - high) * 4 + y),
        device_id_type=MESH,
    )
    cross_mix.start()
    upstream = exchange.wait() + gate_back
    gx[ex] = upstream.astype(BF16)
    dall[own] = (upstream * feat[own, own_cols].astype(F32)).astype(BF16)
    scaled = Push("dp", lambda i: dall.at[pl.ds(pl.multiple_of(i * 128, 128), 128)], ds, dr)
    scaled.send()
    spread_g = Push("expert", lambda i: gx.at[i], hs, hr)
    spread_g.send()

    cross_mix.wait_recv()
    mine = pl.ds(pl.multiple_of(pos * 16, 16), 16)
    total = [mix[t, mine].astype(F32) + mrx[t].astype(F32) for t in range(4)]
    tmx[mine] = jnp.stack(total, axis=1).astype(BF16)
    spread_mix = Wide(
        lambda yp, h: tmx.at[pl.ds(pl.multiple_of(yp * 32 + h * 16, 16), 16)], ws, wr
    )
    spread_mix.send_x()
    lax.fori_loop(2, 4, weight_down, 0)
    spread_mix.wait_x()
    spread_mix.send_a()
    scaled.wait()
    half = pl.ds(pl.multiple_of(c * 512, 512), 512)
    crs[pos, c] = dot(dall[...], feat[:, half], TN).T.astype(BF16)
    spread_c = Push("expert", lambda i: crs.at[lax.rem(i, 4) * 2 + i // 4, c], vs, vr)
    spread_c.send()
    bias_row = jnp.sum(dall[...].astype(F32), axis=0, keepdims=True)
    biases[ex] = jnp.broadcast_to(bias_row, (8, 128))
    spread_b = Push("expert", lambda i: biases.at[i], zs, zr)
    spread_b.send()

    shares = []

    def share(i, k):
        where = lax.rem(i, 4) * 2 + i // 4
        cp = pltpu.make_async_remote_copy(
            src_ref=crs.at[where, c],
            dst_ref=crs.at[where, c],
            send_sem=ks.at[k],
            recv_sem=kr.at[k],
            device_id=partner,
            device_id_type=MESH,
        )
        cp.start()
        shares.append(cp)

    share(ex, 0)
    for i in range(8):
        dst = dgrad_out.at[i // 4, pl.ds(i % 4 * 128, 128)]
        cp = pltpu.make_async_copy(crecv.at[1, i], dst, wgrad_sem.at[i])
        cp.start()
        outs.append(cp)
    lax.fori_loop(0, 1, weight_up, 0)
    spread_mix.wait_a()
    spread_mix.send_b()
    lax.fori_loop(1, 2, weight_up, 0)
    spread_g.wait()
    for i in range(8):
        where = (i % 4) * 2 + i // 4
        cols = pl.ds(where * 128, 128)
        grad = gx[i].astype(F32)
        gf[:, cols] = grad
        dus[:, cols] = (grad * feat_in[:, cols].astype(F32)).astype(BF16)
    for n in range(2):
        cols = pl.ds(n * 512, 512)
        update = dot(feat_in[...], wc[:, cols], NN) + bias_in[:, cols]
        grad = gf[:, cols] + dot(dus[...], wc[cols, :], NT) + gf[:, cols] * update
        fgs[:, cols] = grad.astype(BF16)
    lax.fori_loop(2, 4, weight_up, 0)
    for i in range(8):
        for part_half in range(2):
            dst = ugrad_out.at[i // 4, pl.ds(i % 4 * 256 + part_half * 128, 128)]
            src = part.at[1, i, c, :, pl.ds(part_half * 512, 512)]
            cp = pltpu.make_async_copy(src, dst, wgrad_sem.at[8 + i * 2 + part_half])
            cp.start()
            outs.append(cp)
    logits.wait()
    ordered = dot(order_in[...].astype(BF16), lall[...].astype(BF16), NN).astype(BF16)
    gts[...] = dot(ordered, shared[...], NN)
    sums = jnp.broadcast_to(jnp.sum(lall[...], axis=1, keepdims=True), (64, 128))
    sums = lax.dot_general(
        order_in[...], sums, (NN, ((), ())),
        precision=lax.Precision.HIGHEST, preferred_element_type=F32,
    )
    ost[...] = sums.T[:1]
    for i, (src, dst) in enumerate(((gts, gating_out), (ost, offset_out), (fgs, fgrad_out))):
        cp = pltpu.make_async_copy(src, dst, out_sem.at[i])
        cp.start()
        outs.append(cp)
    def write(source, core, k):
        where = lax.rem(source, 4) * 2 + source // 4
        dst = cross_out.at[
            pl.ds(pl.multiple_of(core * 512, 512), 512),
            pl.ds(pl.multiple_of(where * 128, 128), 128),
        ]
        cp = pltpu.make_async_copy(crs.at[where, core], dst, wgrad_sem.at[24 + k])
        cp.start()
        outs.append(cp)

    write(ex, c, 0)
    for k in range(1, 8):
        source = lax.rem(ex + 8 - k, 8)
        spread_c.copy(source, k, source).wait_recv()
        share(source, k)
        write(source, c, k)
    spread_mix.wait_b()
    cp = pltpu.make_async_copy(tmx, mixed_out, out_sem.at[3])
    cp.start()
    outs.append(cp)
    spread_b.wait()
    for i in range(8):
        where = (i % 4) * 2 + i // 4
        bst[:, pl.ds(where * 128, 128)] = biases[i, :1]
    cp = pltpu.make_async_copy(bst, bias_out, out_sem.at[4])
    cp.start()
    outs.append(cp)
    for k in range(8):
        source = lax.rem(ex + 8 - k, 8)
        where = lax.rem(source, 4) * 2 + source // 4
        pltpu.make_async_remote_copy(
            src_ref=crs.at[where, 1 - c],
            dst_ref=crs.at[where, 1 - c],
            send_sem=ks.at[k],
            recv_sem=kr.at[k],
            device_id=partner,
            device_id_type=MESH,
        ).wait_recv()
        write(source, 1 - c, 8 + k)
    for item in (first, *second, mixer, spread_mix, *backs, exchange, parts, logits, scaled):
        item.drain()
    for item in (spread_g, spread_c, spread_b):
        item.drain()
    for swap in swaps:
        swap.wait_send()
    cross_mix.wait_send()
    for cp in shares:
        cp.wait_send()
    for cp in outs:
        cp.wait()


def core(features, cross_weight, cross_bias, up_weight, down_weight, *tail):
    rows, width = features.shape
    exp_dev, _, hid = up_weight.shape
    every = 16 * rows
    tasks = tail[0].shape[1]
    anywhere = pl.BlockSpec(memory_space=pl.ANY)
    inside = pl.BlockSpec(memory_space=pltpu.VMEM)
    dma = pltpu.SemaphoreType.DMA

    def pairs(*counts):
        return [dma(n if isinstance(n, tuple) else (n,)) for n in counts for _ in range(2)]

    vmem = pltpu.VMEM
    return pl.pallas_call(
        expert_kernel,
        out_shape=(
            jax.ShapeDtypeStruct((rows, tasks, width), BF16),
            jax.ShapeDtypeStruct((rows, width), BF16),
            jax.ShapeDtypeStruct(up_weight.shape, BF16),
            jax.ShapeDtypeStruct(down_weight.shape, BF16),
            jax.ShapeDtypeStruct((width, width), BF16),
            jax.ShapeDtypeStruct((1, width), F32),
            jax.ShapeDtypeStruct((64, width), F32),
            jax.ShapeDtypeStruct((1, 64), F32),
        ),
        in_specs=[inside, anywhere, inside, anywhere, anywhere] + [inside] * 4,
        out_specs=[anywhere] * 8,
        scratch_shapes=[
            vmem((every, width), BF16),
            vmem((every, width), BF16),
            vmem((exp_dev, every, width), BF16),
            vmem((width, width), BF16),
            vmem(up_weight.shape, BF16),
            vmem(down_weight.shape, BF16),
            vmem((exp_dev, every, hid), BF16),
            vmem((exp_dev, every, hid), BF16),
            vmem((exp_dev, 8, 2, rows, width), BF16),
            vmem((exp_dev, 8, rows, width), BF16),
            vmem((exp_dev, rows, width), BF16),
            vmem((exp_dev, 3, rows, width), BF16),
            vmem((exp_dev, 3, rows, width), BF16),
            vmem((exp_dev, rows, width), F32),
            vmem((tasks, rows, width), BF16),
            vmem((2, tasks, 16, width), BF16),
            vmem((2, 2, tasks, 16, width), BF16),
            vmem((tasks, 16, width), BF16),
            vmem((rows, tasks, width), BF16),
            vmem((2, 2, 4, rows, 128), BF16),
            vmem((2, 2, 2, 4, rows, 128), BF16),
            vmem((2, 8, rows, 128), BF16),
            vmem((15, rows, 128), BF16),
            vmem((8, 8, rows), F32),
            vmem((64, every), F32),
            vmem((8, rows, 128), BF16),
            vmem((every, 128), BF16),
            vmem((8, 2, width // 2, 128), BF16),
            vmem((8, 8, 128), F32),
            vmem((rows, width), F32),
            vmem((rows, width), BF16),
            vmem((rows, width), BF16),
            vmem((64, width), F32),
            vmem((1, width), F32),
            vmem((1, 64), F32),
            vmem((8, 8, rows), F32),
            vmem((rows, 128), F32),
            vmem((tasks, rows, width), BF16),
            vmem((64, width), BF16),
            dma((4,)), dma((5,)), dma((40,)),
            *pairs(17, (2, 17), 4, (2, 9)),
            *pairs(6, 7, (2, 6), 15, 1, 7, 15, 7, 15, 7, 8, 7),
            pltpu.SemaphoreType.REGULAR,
        ],
        compiler_params=pltpu.CompilerParams(
            collective_id=0, has_side_effects=True, vmem_limit_bytes=67043328
        ),
        name="step",
    )(features, cross_weight, cross_bias, up_weight, down_weight, *tail)


def local(
    features, cross_weight, cross_bias, gate_weight, gate_offset, up_weight, down_weight, task_grad
):
    tasks = task_grad.shape[1]
    exp_dev = up_weight.shape[0]
    slots = lax.axis_size("expert")
    gates = tasks * slots * exp_dev
    columns = np.arange(gates).reshape(tasks, slots, exp_dev).transpose(1, 2, 0).reshape(-1)
    order = np.zeros((gates, gates), np.float32)
    order[columns, np.arange(gates)] = 1.0
    outs = core(
        features, cross_weight[0], cross_bias, up_weight, down_weight,
        task_grad, gate_weight.T, gate_offset[None], jnp.asarray(order),
    )
    mixed, feature_grad, up_grad, down_grad, cross_grad, bias_grad, gating_grad, offset = outs
    return (
        mixed,
        feature_grad,
        up_grad,
        down_grad,
        cross_grad[None].astype(F32),
        bias_grad,
        gating_grad.T,
        offset.reshape(-1),
    )


def solution(mesh):
    placed = (
        P("dp", None),
        P(),
        P(),
        P(),
        P(),
        P("expert", None, "dp"),
        P("expert", "dp", None),
        P("dp", None, None),
    )
    return jax.shard_map(
        local,
        mesh=mesh,
        in_specs=placed,
        out_specs=(
            P("dp", None, None),
            P("dp", None),
            P("expert", None, "dp"),
            P("expert", "dp", None),
            P(),
            P(),
            P(),
            P(),
        ),
        check_vma=False,
    )
```

```python
import jax
import jax.numpy as jnp
import numpy as np
from jax import lax
from jax.experimental import pallas as pl
from jax.experimental.pallas import tpu as pltpu
from jax.sharding import PartitionSpec as P

F32 = jnp.float32
BF16 = jnp.bfloat16


MESH = pl.DeviceIdType.MESH
THIRDS = ((0, 48), (48, 48), (96, 32))


def place():
    dp, ex = lax.axis_index("dp"), lax.axis_index("expert")
    z, xl, c = dp // 4, lax.rem(dp // 2, 2), lax.rem(dp, 2)

    def rank(dx, dz, core):
        return lax.rem(z + dz + 4, 4) * 4 + (1 - xl if dx else xl) * 2 + core

    return dp, ex, c, rank


class Spread:
    STEPS = (
        ((0, (0, 0)), (1, (0, 0)), (2, (0, 0))),
        ((3, (0, 1)), (4, (0, 1)), (5, (1, 0))),
        ((6, (0, 2)), (7, (1, 1)), (8, (1, -1))),
    )
    GOT = (
        ((0, (1, 0)), (1, (0, 1)), (2, (0, -1))),
        ((3, (1, 1)), (4, (0, 2)), (5, (1, -1))),
        ((6, (1, 2)), (7, (1, 2)), (8, (1, 2))),
    )
    ORDER = ((0, 0), (1, 0), (0, 1), (0, -1), (1, 1), (0, 2), (1, -1), (1, 2))

    def __init__(self, block, own, ssem, rsem):
        self.block, self.own, self.ssem, self.rsem = block, own, ssem, rsem
        self.dp, self.ex, self.c, self.rank = place()
        self.near = (
            self.rank(1, 0, self.c),
            self.rank(0, -1, self.c),
            self.rank(0, 1, self.c),
        )
        self.sent = []

    def copy(self, src, dst, k, to):
        return pltpu.make_async_remote_copy(
            src_ref=src,
            dst_ref=dst,
            send_sem=self.ssem.at[k],
            recv_sem=self.rsem.at[k],
            device_id=(to, self.ex),
            device_id_type=MESH,
        )

    def send(self, step):
        for i, (k, rel) in enumerate(self.STEPS[step]):
            part = THIRDS[i] if step == 2 else (0, 128)
            dst = self.block(self.rank(*rel, self.c), *part)
            src = self.own if step == 0 else dst
            cp = self.copy(src, dst, k, self.near[i])
            cp.start()
            self.sent.append(cp)

    def wait(self, step):
        for i, (k, rel) in enumerate(self.GOT[step]):
            part = THIRDS[i] if step == 2 else (0, 128)
            dst = self.block(self.rank(*rel, self.c), *part)
            self.copy(dst, dst, k, self.near[i]).wait_recv()

    def share(self, lo, hi):
        for j in range(lo, hi):
            dst = self.block(self.rank(*self.ORDER[j], self.c), 0, 128)
            cp = self.copy(self.own if j == 0 else dst, dst, 9 + j, self.rank(0, 0, 1 - self.c))
            cp.start()
            self.sent.append(cp)

    def wait_shared(self, lo=0, hi=8):
        for j in range(lo, hi):
            dst = self.block(self.rank(*self.ORDER[j], 1 - self.c), 0, 128)
            self.copy(dst, dst, 9 + j, self.rank(0, 0, 1 - self.c)).wait_recv()

    def drain(self):
        for cp in self.sent:
            cp.wait_send()


class Gather:
    def __init__(self, block, ra, rb, rc, ssem, rsem):
        self.block, self.ra, self.rb, self.rc = block, ra, rb, rc
        self.ssem, self.rsem = ssem, rsem
        self.dp, self.ex, self.c, self.rank = place()
        self.x = self.rank(1, 0, self.c)
        self.up = self.rank(0, 1, self.c)
        self.down = self.rank(0, -1, self.c)
        self.sent = []

    def ref(self, dx, dz):
        return self.block(self.rank(dx, dz, 0) // 2)

    def copy(self, src, dst, k, to):
        return pltpu.make_async_remote_copy(
            src_ref=src,
            dst_ref=dst,
            send_sem=self.ssem.at[k],
            recv_sem=self.rsem.at[k],
            device_id=(to, self.ex),
            device_id_type=MESH,
        )

    def go(self, src, dst, k, to):
        cp = self.copy(src, dst, k, to)
        cp.start()
        self.sent.append(cp)

    def add(self, ref, got):
        ref[...] = (ref[...].astype(F32) + got[...].astype(F32)).astype(BF16)

    def send_a(self):
        for i, to in enumerate((self.x, self.up, self.down)):
            rows = pl.ds(*THIRDS[i])
            self.go(self.ref(1, 2).at[rows], self.ra.at[rows], i, to)

    def wait_a(self):
        for i, rel in enumerate(((0, 2), (1, 1), (1, -1))):
            rows = pl.ds(*THIRDS[i])
            got = self.ra.at[rows]
            self.copy(got, got, i, self.x).wait_recv()
            self.add(self.ref(*rel).at[rows], got)

    def send_b(self):
        self.go(self.ref(1, 1), self.rb.at[1], 4, self.x)
        self.go(self.ref(0, 2), self.rb.at[0], 3, self.up)
        self.go(self.ref(1, -1), self.rb.at[2], 5, self.down)

    def wait_b(self):
        for i, rel in enumerate(((0, 1), (0, 1), (1, 0))):
            got = self.rb.at[i]
            self.copy(got, got, 3 + i, self.x).wait_recv()
            self.add(self.ref(*rel), got)

    def send_c(self):
        self.go(self.ref(1, 0), self.rc.at[0], 6, self.x)
        self.go(self.ref(0, 1), self.rc.at[1], 7, self.up)
        self.go(self.ref(0, -1), self.rc.at[2], 8, self.down)

    def wait_c(self):
        total = self.ref(0, 0)[...].astype(F32)
        for i in range(3):
            got = self.rc.at[i]
            self.copy(got, got, 6 + i, self.x).wait_recv()
            total = total + got[...].astype(F32)
        return total

    def drain(self):
        for cp in self.sent:
            cp.wait_send()


class Sides:
    def __init__(self, ref, ssem, rsem):
        self.ref, self.ssem, self.rsem = ref, ssem, rsem
        self.dp, ex = lax.axis_index("dp"), lax.axis_index("expert")
        self.y, self.h = lax.rem(ex, 4), ex // 4
        self.other = (1 - self.h) * 4 + self.y
        self.up = self.h * 4 + lax.rem(self.y + 1, 4)
        self.down = self.h * 4 + lax.rem(self.y + 3, 4)
        self.sent = []

    def at(self, dy, h):
        return self.ref(lax.rem(self.y + dy + 4, 4), h)

    def copy(self, src, dst, k, to):
        return pltpu.make_async_remote_copy(
            src_ref=src,
            dst_ref=dst,
            send_sem=self.ssem.at[k],
            recv_sem=self.rsem.at[k],
            device_id=(self.dp, to),
            device_id_type=MESH,
        )

    def go(self, src, dst, k, to):
        cp = self.copy(src, dst, k, to)
        cp.start()
        self.sent.append(cp)

    def got(self, dst, k):
        self.copy(dst, dst, k, self.other).wait_recv()

    def drain(self):
        for cp in self.sent:
            cp.wait_send()


class Wide(Sides):
    def send_x(self):
        self.go(self.at(0, self.h), self.at(0, self.h), 0, self.other)

    def wait_x(self):
        self.got(self.at(0, 1 - self.h), 0)

    def send_a(self):
        for h in range(2):
            self.go(self.at(0, h), self.at(0, h), 1 + h, self.down)
            self.go(self.at(0, h), self.at(0, h), 3 + h, self.up)

    def wait_a(self):
        for h in range(2):
            self.got(self.at(1, h), 1 + h)
            self.got(self.at(-1, h), 3 + h)

    def send_b(self):
        self.go(self.at(1, 0), self.at(1, 0), 5, self.down)
        self.go(self.at(-1, 1), self.at(-1, 1), 6, self.up)

    def wait_b(self):
        for h in range(2):
            self.got(self.at(2, h), 5 + h)


class Narrow(Sides):
    def __init__(self, ref, ra, rb, ssem, rsem):
        super().__init__(ref, ssem, rsem)
        self.ra, self.rb = ra, rb

    def send_a(self):
        self.go(self.at(2, 0), self.ra.at[0], 0, self.up)
        self.go(self.at(2, 1), self.ra.at[1], 1, self.down)

    def wait_a(self):
        for h, dy in enumerate((1, -1)):
            self.got(self.ra.at[h], h)
            ref, got = self.at(dy, h), self.ra.at[h]

            def add(k, carry):
                ref[k] = (ref[k].astype(F32) + got[k].astype(F32)).astype(BF16)
                return carry

            lax.fori_loop(0, got.shape[0], add, 0)

    def send_b(self):
        for h in range(2):
            self.go(self.at(1, h), self.rb.at[0, h], 2 + h, self.up)
            self.go(self.at(-1, h), self.rb.at[1, h], 4 + h, self.down)

    def wait_b(self, put):
        for h in range(2):
            for d in range(2):
                self.got(self.rb.at[d, h], 2 + 2 * d + h)
            ref = self.at(0, h)

            def add(k, carry):
                total = ref[k].astype(F32) + self.rb[0, h, k].astype(F32)
                put(k, h, (total + self.rb[1, h, k].astype(F32)).astype(BF16))
                return carry

            lax.fori_loop(0, ref.shape[0], add, 0)


class Push:
    def __init__(self, axis, slot, ssem, rsem):
        self.slot, self.ssem, self.rsem = slot, ssem, rsem
        self.n, self.me = lax.axis_size(axis), lax.axis_index(axis)
        if axis == "dp":
            other = lax.axis_index("expert")
            self.to = lambda k: (k, other)
        else:
            other = lax.axis_index("dp")
            self.to = lambda k: (other, k)
        self.sent = []

    def copy(self, i, k, to):
        return pltpu.make_async_remote_copy(
            src_ref=self.slot(i),
            dst_ref=self.slot(i),
            send_sem=self.ssem.at[k - 1],
            recv_sem=self.rsem.at[k - 1],
            device_id=self.to(to),
            device_id_type=MESH,
        )

    def send(self):
        for k in range(1, self.n):
            cp = self.copy(self.me, k, lax.rem(self.me + k, self.n))
            cp.start()
            self.sent.append(cp)

    def wait(self):
        for k in range(1, self.n):
            source = lax.rem(self.me + self.n - k, self.n)
            self.copy(source, k, source).wait_recv()

    def drain(self):
        for cp in self.sent:
            cp.wait_send()


def dot(a, b, dims):
    return lax.dot_general(a, b, (dims, ((), ())), preferred_element_type=F32)


NN, NT, TN = ((1,), (0,)), ((1,), (1,)), ((0,), (0,))


class Exchange:
    def __init__(self, block, got, ssem, rsem):
        self.block, self.got, self.ssem, self.rsem = block, got, ssem, rsem
        dp, ex = lax.axis_index("dp"), lax.axis_index("expert")
        self.chip, self.c, self.y, self.h = dp // 2, lax.rem(dp, 2), lax.rem(ex, 4), ex // 4
        self.sent = []

    def place(self, j):
        chip = lax.rem(self.chip + j % 8, 8)
        return chip, (1 - self.h if j >= 8 else self.h)

    def copy(self, j):
        chip, h = self.place(j)
        return pltpu.make_async_remote_copy(
            src_ref=self.block(chip, h),
            dst_ref=self.got.at[j - 1],
            send_sem=self.ssem.at[j - 1],
            recv_sem=self.rsem.at[j - 1],
            device_id=(chip * 2 + self.c, h * 4 + self.y),
            device_id_type=MESH,
        )

    def send(self):
        for j in range(1, 16):
            cp = self.copy(j)
            cp.start()
            self.sent.append(cp)

    def wait(self):
        total = self.block(self.chip, self.h)[...].astype(F32)
        for j in range(1, 16):
            self.copy(j).wait_recv()
            total = total + self.got[j - 1].astype(F32)
        return total

    def drain(self):
        for cp in self.sent:
            cp.wait_send()


def expert_kernel(
    feat_in, wc_in, bias_in, up_in, down_in, tg_in, gate_in, gate_off, order_in,
    mixed_out, fgrad_out, ugrad_out, dgrad_out, cross_out, bias_out, gating_out, offset_out,
    feat, shared, og, wc, up, down, act, dsl, part, crecv, ra, rb, rc, group,
    mix, mra, mrb, mrx, tmx, bra, brb, bt, got, gp, lall, gx, dall, crs, biases,
    gf, dus, fgs, gts, bst, ost, gates_all, gates_own, tg, gate_w,
    load_sem, out_sem, wgrad_sem, fs, fr, gs, gr, cs, cr, ts, tr,
    ms, mr, ws, wr, bs, br, us, ur, xs, xr, ps, pr, ls, lr, hs, hr, ds, dr, vs, vr, ks, kr, zs, zr,
    free,
):
    dp, ex, c, rank = place()
    z, xl = dp // 4, lax.rem(dp // 2, 2)
    y, high = lax.rem(ex, 4), ex // 4
    barrier = pltpu.get_barrier_semaphore()
    for k in range(1, 16):
        to = (lax.rem(dp + k, 16), ex)
        pl.semaphore_signal(barrier, inc=1, device_id=to, device_id_type=MESH)
    for k in range(1, 8):
        to = (dp, lax.rem(ex + k, 8))
        pl.semaphore_signal(barrier, inc=1, device_id=to, device_id_type=MESH)
    for k in range(1, 8):
        to = (lax.rem(dp // 2 + k, 8) * 2 + c, (1 - high) * 4 + y)
        pl.semaphore_signal(barrier, inc=1, device_id=to, device_id_type=MESH)
    loads = [
        pltpu.make_async_copy(src, dst, load_sem.at[i])
        for i, (src, dst) in enumerate((
            (feat_in, feat.at[pl.ds(dp * 128, 128)]),
            (wc_in, wc), (up_in, up), (down_in, down),
        ))
    ]
    for cp in loads:
        cp.start()
    pl.semaphore_wait(barrier, 29)
    partner = (rank(0, 0, 1 - c), ex)
    first = Spread(lambda d, r, n: feat.at[pl.ds(d * 128 + r, n)], feat_in, fs, fr)
    second = [
        Spread(
            lambda d, r, n, e=e: og.at[e, pl.ds(d * 128 + r, n)],
            og.at[e, pl.ds(dp * 128, 128)], gs.at[e], gr.at[e],
        )
        for e in range(2)
    ]
    first.send(0)
    first.share(0, 1)
    for cp in loads:
        cp.wait()
    for t in range(4):
        tg[t] = tg_in[:, t, :]
    own = pl.ds(pl.multiple_of(dp * 128, 128), 128)
    base = feat_in[...].astype(F32)
    update = dot(feat_in[...], wc[...], NN) + bias_in[...]
    fgs[...] = (base * update + base).astype(BF16)
    gate_w[...] = dot(order_in[...].astype(BF16), gate_in[...], TN).astype(BF16)
    offsets = lax.dot_general(
        order_in[...], jnp.broadcast_to(gate_off[...], (128, 64)), (((0,), (1,)), ((), ())),
        precision=lax.Precision.HIGHEST, preferred_element_type=F32,
    )
    expo = jnp.exp(dot(gate_w[...], fgs[...], NT) + offsets)
    for i in range(8):
        gates_all[i] = expo[i * 8 : i * 8 + 8]
    total = gates_all[0]
    for i in range(1, 8):
        total = total + gates_all[i]
    total = total + pltpu.roll(total, 4, 0)
    for i in range(8):
        gates_all[i] = gates_all[i] / total
    gates_own[...] = jnp.zeros((128, 128), F32)
    gates_own[:8] = gates_all[ex]
    gates_own[...] = gates_own[...].T
    for e in range(2):
        total = gates_own[:, e * 4 : e * 4 + 1] * tg[0].astype(F32)
        for t in range(1, 4):
            total = total + gates_own[:, e * 4 + t : e * 4 + t + 1] * tg[t].astype(F32)
        og[e, own] = total.astype(BF16)

    def hidden(i, carry):
        dx = jnp.where((i == 1) | (i == 4) | (i == 6) | (i == 7), 1, 0)
        dz = jnp.where((i == 5) | (i == 7), 2, jnp.where((i == 3) | (i == 6), 3, 0))
        dz = jnp.where((i == 2) | (i == 4), 1, dz)
        chip = lax.rem(z + dz, 4) * 2 + xl + dx - 2 * xl * dx
        rows = pl.ds(pl.multiple_of(chip * 256, 256), 256)
        for n in range(2):
            cols = pl.ds(n * 512, 512)
            base = feat[rows, cols].astype(F32)
            update = dot(feat[rows, :], wc[:, cols], NN) + bias_in[:, cols]
            shared[rows, cols] = (base * update + base).astype(BF16)
        for e in range(2):
            pre = dot(shared[rows, :], up[e], NN)
            sig = jax.nn.sigmoid(pre)
            act[e, rows] = (pre * sig).astype(BF16)
            dsl[e, rows] = (sig * (1.0 + pre * (1.0 - sig))).astype(BF16)
        return carry

    first.wait_shared(0, 1)
    lax.fori_loop(0, 1, hidden, 0)
    first.wait(0)
    first.send(1)
    first.share(1, 4)
    second[0].send(0)
    second[0].share(0, 1)
    first.wait_shared(1, 4)
    lax.fori_loop(1, 4, hidden, 0)
    first.wait(1)
    first.send(2)
    first.share(4, 7)
    second[1].send(0)
    second[1].share(0, 1)
    first.wait_shared(4, 7)
    lax.fori_loop(4, 7, hidden, 0)
    first.wait(2)
    first.share(7, 8)
    second[0].wait(0)
    second[0].send(1)
    second[0].share(1, 4)
    first.wait_shared(7, 8)
    lax.fori_loop(7, 8, hidden, 0)

    outs = []
    swaps = []
    trees = []
    for e in range(2):
        def forward(k, carry):
            rows = pl.ds(pl.multiple_of(k * 256, 256), 256)
            for n in range(2):
                cols = pl.ds(n * 512, 512)
                out = dot(act[e, rows], down[e, :, cols], NN).astype(BF16)
                part[e, k, 0, :, cols] = out[:128]
                part[e, k, 1, :, cols] = out[128:]
            return carry

        lax.fori_loop(0, 8, forward, 0)
        swap = pltpu.make_async_remote_copy(
            src_ref=part.at[e, :, 1 - c],
            dst_ref=crecv.at[e],
            send_sem=cs.at[e],
            recv_sem=cr.at[e],
            device_id=partner,
            device_id_type=MESH,
        )
        swap.start()
        swaps.append(swap)
        blocks = lambda k, e=e: part.at[e, k, c]
        trees.append(Gather(blocks, ra.at[e], rb.at[e], rc.at[e], ts.at[e], tr.at[e]))
        if e == 0:
            second[1].wait(0)
            second[1].send(1)
            second[1].share(1, 4)
    second[0].wait(1)
    second[0].send(2)
    second[0].share(4, 7)
    for e in range(2):
        swaps[e].wait_recv()

        def merge(k, carry):
            part[e, k, c] = (part[e, k, c].astype(F32) + crecv[e, k].astype(F32)).astype(BF16)
            return carry

        lax.fori_loop(0, 8, merge, 0)
        if e == 0:
            pl.semaphore_signal(free, inc=1, device_id=partner, device_id_type=MESH)
            second[1].wait(1)
            second[1].send(2)
            second[1].share(4, 7)
        trees[e].send_a()
    second[0].wait(2)
    second[0].share(7, 8)
    second[0].wait_shared()

    def backward(k, carry):
        rows = pl.ds(pl.multiple_of(k * 256, 256), 256)
        grad = dot(og[0, rows], down[0], NT)
        dsl[0, rows] = (grad * dsl[0, rows].astype(F32)).astype(BF16)
        return carry

    lax.fori_loop(0, 8, backward, 0)
    second[1].wait(2)
    second[1].share(7, 8)
    for e in range(2):
        trees[e].wait_a()
        trees[e].send_b()
        swaps[e].wait_send()
    second[1].wait_shared()
    pl.semaphore_wait(free, 1)

    def to_shared(k, carry):
        rows = pl.ds(pl.multiple_of(k * 256, 256), 256)
        grad = dot(og[1, rows], down[1], NT)
        dsl[1, rows] = (grad * dsl[1, rows].astype(F32)).astype(BF16)
        for n in range(2):
            cols = pl.ds(n * 512, 512)
            grad = dot(dsl[0, rows], up[0, cols], NT) + dot(dsl[1, rows], up[1, cols], NT)
            part[1 - c, k, 1 - c, :, cols] = grad[:128].astype(BF16)
            part[c, k, 1 - c, :, cols] = grad[128:].astype(BF16)
        return carry

    swaps = []
    backs = []
    for i in range(2):
        lax.fori_loop(i * 4, i * 4 + 4, to_shared, 0)
        swap = pltpu.make_async_remote_copy(
            src_ref=part.at[0, pl.ds(i * 4, 4), 1 - c],
            dst_ref=crecv.at[0, pl.ds(i * 4, 4)],
            send_sem=cs.at[2 + i],
            recv_sem=cr.at[2 + i],
            device_id=partner,
            device_id_type=MESH,
        )
        swap.start()
        swaps.append(swap)
    for i in range(2):
        swaps[i].wait_recv()

        def merge_back(k, carry):
            total = part[1, k, 1 - c].astype(F32) + crecv[0, k].astype(F32)
            part[1, k, 1 - c] = total.astype(BF16)
            return carry

        lax.fori_loop(i * 4, i * 4 + 4, merge_back, 0)
        back = Narrow(
            lambda yp, h, i=i: part.at[
                1, pl.ds(i * 4, 4), 1 - c, :, pl.ds(pl.multiple_of(yp * 256 + h * 128, 128), 128)
            ],
            bra.at[i], brb.at[i], bs.at[i], br.at[i],
        )
        back.send_a()
        backs.append(back)
        trees[i].wait_b()
        trees[i].send_c()

    def weight_down(i, carry):
        e, m = i // 2, lax.rem(i, 2)
        cols = pl.ds(pl.multiple_of(m * 256, 256), 256)
        tile = dot(act[e, :, cols], og[e], TN).astype(BF16)
        crecv[1, i * 2] = tile[:128]
        crecv[1, i * 2 + 1] = tile[128:]
        return carry

    def weight_up(m, carry):
        cols = pl.ds(pl.multiple_of(m * 256, 256), 256)
        for e in range(2):
            tile = dot(shared[:, cols], dsl[e], TN).astype(BF16)
            part[1, e * 4 + m, c, :, :512] = tile[:128]
            part[1, e * 4 + m, c, :, 512:] = tile[128:]
        return carry

    for back in backs:
        back.wait_a()
        back.send_b()
    lax.fori_loop(0, 1, weight_down, 0)
    group[0] = trees[0].wait_c()
    group[1] = trees[1].wait_c()
    trees[0].drain()
    trees[1].drain()

    pos = y * 2 + high
    own_cols = pl.ds(pl.multiple_of(pos * 128, 128), 128)
    lane = lax.broadcasted_iota(jnp.int32, (128, 128), 1)
    packed = jnp.zeros((128, 128), F32)
    for e in range(2):
        for t in range(4):
            inner = jnp.sum(tg[t].astype(F32) * group[e], axis=1, keepdims=True)
            packed = packed + jnp.where(lane == e * 4 + t, inner, 0.0)
    gp[ex] = packed.T[:8]
    parts = Push("expert", lambda i: gp.at[i], ps, pr)
    parts.send()
    for t in range(4):
        mix[t] = (
            gates_own[:, t : t + 1] * group[0] + gates_own[:, t + 4 : t + 5] * group[1]
        ).astype(BF16)
    mixer = Narrow(
        lambda yp, h: mix.at[:, pl.ds(pl.multiple_of(yp * 32 + h * 16, 16), 16)], mra, mrb, ms, mr
    )
    mixer.send_a()

    for i in range(2):
        def keep_back(k, h, total):
            bt[h, i * 4 + k] = total

        backs[i].wait_b(keep_back)
    exchange = Exchange(lambda k, h: bt.at[h, k], got, us, ur)
    exchange.send()
    mixer.wait_a()
    mixer.send_b()
    parts.wait()
    weighed = [gates_all[i] * gp[i] for i in range(8)]
    total = sum(weighed[1:], weighed[0])
    total = total + pltpu.roll(total, 4, 0)
    for i in range(8):
        lall[pl.ds(i * 8, 8), own] = gates_all[i] * (gp[i] - total)
    logits = Push("dp", lambda i: lall.at[:, pl.ds(pl.multiple_of(i * 128, 128), 128)], ls, lr)
    gate_back = dot(lall[:, own].astype(BF16), gate_w[:, own_cols], TN)
    lax.fori_loop(1, 2, weight_down, 0)
    def keep_mix(k, h, total):
        mix[k, pl.ds(pl.multiple_of(y * 32 + h * 16, 16), 16)] = total

    mixer.wait_b(keep_mix)
    cross_mix = pltpu.make_async_remote_copy(
        src_ref=mixer.at(0, 1 - high),
        dst_ref=mrx,
        send_sem=xs.at[0],
        recv_sem=xr.at[0],
        device_id=(dp, (1 - high) * 4 + y),
        device_id_type=MESH,
    )
    cross_mix.start()
    upstream = exchange.wait() + gate_back
    gx[ex] = upstream.astype(BF16)
    dall[own] = (upstream * feat[own, own_cols].astype(F32)).astype(BF16)
    scaled = Push("dp", lambda i: dall.at[pl.ds(pl.multiple_of(i * 128, 128), 128)], ds, dr)
    scaled.send()
    spread_g = Push("expert", lambda i: gx.at[i], hs, hr)
    spread_g.send()

    cross_mix.wait_recv()
    mine = pl.ds(pl.multiple_of(pos * 16, 16), 16)
    total = [mix[t, mine].astype(F32) + mrx[t].astype(F32) for t in range(4)]
    tmx[mine] = jnp.stack(total, axis=1).astype(BF16)
    spread_mix = Wide(
        lambda yp, h: tmx.at[pl.ds(pl.multiple_of(yp * 32 + h * 16, 16), 16)], ws, wr
    )
    spread_mix.send_x()
    lax.fori_loop(2, 4, weight_down, 0)
    spread_mix.wait_x()
    spread_mix.send_a()
    scaled.wait()
    half = pl.ds(pl.multiple_of(c * 512, 512), 512)
    crs[pos, c] = dot(dall[...], feat[:, half], TN).T.astype(BF16)
    spread_c = Push("expert", lambda i: crs.at[lax.rem(i, 4) * 2 + i // 4, c], vs, vr)
    spread_c.send()
    bias_row = jnp.sum(dall[...].astype(F32), axis=0, keepdims=True)
    biases[ex] = jnp.broadcast_to(bias_row, (8, 128))
    spread_b = Push("expert", lambda i: biases.at[i], zs, zr)
    spread_b.send()
    logits.send()

    shares = []

    def share(i, k):
        where = lax.rem(i, 4) * 2 + i // 4
        cp = pltpu.make_async_remote_copy(
            src_ref=crs.at[where, c],
            dst_ref=crs.at[where, c],
            send_sem=ks.at[k],
            recv_sem=kr.at[k],
            device_id=partner,
            device_id_type=MESH,
        )
        cp.start()
        shares.append(cp)

    share(ex, 0)
    for i in range(8):
        dst = dgrad_out.at[i // 4, pl.ds(i % 4 * 128, 128)]
        cp = pltpu.make_async_copy(crecv.at[1, i], dst, wgrad_sem.at[i])
        cp.start()
        outs.append(cp)
    lax.fori_loop(0, 1, weight_up, 0)
    spread_mix.wait_a()
    spread_mix.send_b()
    lax.fori_loop(1, 2, weight_up, 0)
    spread_g.wait()
    for i in range(8):
        where = (i % 4) * 2 + i // 4
        cols = pl.ds(where * 128, 128)
        grad = gx[i].astype(F32)
        gf[:, cols] = grad
        dus[:, cols] = (grad * feat_in[:, cols].astype(F32)).astype(BF16)
    for n in range(2):
        cols = pl.ds(n * 512, 512)
        update = dot(feat_in[...], wc[:, cols], NN) + bias_in[:, cols]
        grad = gf[:, cols] + dot(dus[...], wc[cols, :], NT) + gf[:, cols] * update
        fgs[:, cols] = grad.astype(BF16)
    lax.fori_loop(2, 4, weight_up, 0)
    for i in range(8):
        for part_half in range(2):
            dst = ugrad_out.at[i // 4, pl.ds(i % 4 * 256 + part_half * 128, 128)]
            src = part.at[1, i, c, :, pl.ds(part_half * 512, 512)]
            cp = pltpu.make_async_copy(src, dst, wgrad_sem.at[8 + i * 2 + part_half])
            cp.start()
            outs.append(cp)
    logits.wait()
    ordered = dot(order_in[...].astype(BF16), lall[...].astype(BF16), NN).astype(BF16)
    gts[...] = dot(ordered, shared[...], NN)
    sums = jnp.broadcast_to(jnp.sum(lall[...], axis=1, keepdims=True), (64, 128))
    sums = lax.dot_general(
        order_in[...], sums, (NN, ((), ())),
        precision=lax.Precision.HIGHEST, preferred_element_type=F32,
    )
    ost[...] = sums.T[:1]
    for i, (src, dst) in enumerate(((gts, gating_out), (ost, offset_out), (fgs, fgrad_out))):
        cp = pltpu.make_async_copy(src, dst, out_sem.at[i])
        cp.start()
        outs.append(cp)
    def write(source, core, k):
        where = lax.rem(source, 4) * 2 + source // 4
        dst = cross_out.at[
            pl.ds(pl.multiple_of(core * 512, 512), 512),
            pl.ds(pl.multiple_of(where * 128, 128), 128),
        ]
        cp = pltpu.make_async_copy(crs.at[where, core], dst, wgrad_sem.at[24 + k])
        cp.start()
        outs.append(cp)

    write(ex, c, 0)
    for k in range(1, 8):
        source = lax.rem(ex + 8 - k, 8)
        spread_c.copy(source, k, source).wait_recv()
        share(source, k)
        write(source, c, k)
    spread_mix.wait_b()
    cp = pltpu.make_async_copy(tmx, mixed_out, out_sem.at[3])
    cp.start()
    outs.append(cp)
    spread_b.wait()
    for i in range(8):
        where = (i % 4) * 2 + i // 4
        bst[:, pl.ds(where * 128, 128)] = biases[i, :1]
    cp = pltpu.make_async_copy(bst, bias_out, out_sem.at[4])
    cp.start()
    outs.append(cp)
    for k in range(8):
        source = lax.rem(ex + 8 - k, 8)
        where = lax.rem(source, 4) * 2 + source // 4
        pltpu.make_async_remote_copy(
            src_ref=crs.at[where, 1 - c],
            dst_ref=crs.at[where, 1 - c],
            send_sem=ks.at[k],
            recv_sem=kr.at[k],
            device_id=partner,
            device_id_type=MESH,
        ).wait_recv()
        write(source, 1 - c, 8 + k)
    for item in (first, *second, mixer, spread_mix, *backs, exchange, parts, logits, scaled):
        item.drain()
    for item in (spread_g, spread_c, spread_b):
        item.drain()
    for swap in swaps:
        swap.wait_send()
    cross_mix.wait_send()
    for cp in shares:
        cp.wait_send()
    for cp in outs:
        cp.wait()


def core(features, cross_weight, cross_bias, up_weight, down_weight, *tail):
    rows, width = features.shape
    exp_dev, _, hid = up_weight.shape
    every = 16 * rows
    tasks = tail[0].shape[1]
    anywhere = pl.BlockSpec(memory_space=pl.ANY)
    inside = pl.BlockSpec(memory_space=pltpu.VMEM)
    dma = pltpu.SemaphoreType.DMA

    def pairs(*counts):
        return [dma(n if isinstance(n, tuple) else (n,)) for n in counts for _ in range(2)]

    vmem = pltpu.VMEM
    return pl.pallas_call(
        expert_kernel,
        out_shape=(
            jax.ShapeDtypeStruct((rows, tasks, width), BF16),
            jax.ShapeDtypeStruct((rows, width), BF16),
            jax.ShapeDtypeStruct(up_weight.shape, BF16),
            jax.ShapeDtypeStruct(down_weight.shape, BF16),
            jax.ShapeDtypeStruct((width, width), BF16),
            jax.ShapeDtypeStruct((1, width), F32),
            jax.ShapeDtypeStruct((64, width), F32),
            jax.ShapeDtypeStruct((1, 64), F32),
        ),
        in_specs=[inside, anywhere, inside, anywhere, anywhere] + [inside] * 4,
        out_specs=[anywhere] * 8,
        scratch_shapes=[
            vmem((every, width), BF16),
            vmem((every, width), BF16),
            vmem((exp_dev, every, width), BF16),
            vmem((width, width), BF16),
            vmem(up_weight.shape, BF16),
            vmem(down_weight.shape, BF16),
            vmem((exp_dev, every, hid), BF16),
            vmem((exp_dev, every, hid), BF16),
            vmem((exp_dev, 8, 2, rows, width), BF16),
            vmem((exp_dev, 8, rows, width), BF16),
            vmem((exp_dev, rows, width), BF16),
            vmem((exp_dev, 3, rows, width), BF16),
            vmem((exp_dev, 3, rows, width), BF16),
            vmem((exp_dev, rows, width), F32),
            vmem((tasks, rows, width), BF16),
            vmem((2, tasks, 16, width), BF16),
            vmem((2, 2, tasks, 16, width), BF16),
            vmem((tasks, 16, width), BF16),
            vmem((rows, tasks, width), BF16),
            vmem((2, 2, 4, rows, 128), BF16),
            vmem((2, 2, 2, 4, rows, 128), BF16),
            vmem((2, 8, rows, 128), BF16),
            vmem((15, rows, 128), BF16),
            vmem((8, 8, rows), F32),
            vmem((64, every), F32),
            vmem((8, rows, 128), BF16),
            vmem((every, 128), BF16),
            vmem((8, 2, width // 2, 128), BF16),
            vmem((8, 8, 128), F32),
            vmem((rows, width), F32),
            vmem((rows, width), BF16),
            vmem((rows, width), BF16),
            vmem((64, width), F32),
            vmem((1, width), F32),
            vmem((1, 64), F32),
            vmem((8, 8, rows), F32),
            vmem((rows, 128), F32),
            vmem((tasks, rows, width), BF16),
            vmem((64, width), BF16),
            dma((4,)), dma((5,)), dma((40,)),
            *pairs(17, (2, 17), 4, (2, 9)),
            *pairs(6, 7, (2, 6), 15, 1, 7, 15, 7, 15, 7, 8, 7),
            pltpu.SemaphoreType.REGULAR,
        ],
        compiler_params=pltpu.CompilerParams(
            collective_id=0, has_side_effects=True, vmem_limit_bytes=67043328
        ),
        name="step",
    )(features, cross_weight, cross_bias, up_weight, down_weight, *tail)


def local(
    features, cross_weight, cross_bias, gate_weight, gate_offset, up_weight, down_weight, task_grad
):
    tasks = task_grad.shape[1]
    exp_dev = up_weight.shape[0]
    slots = lax.axis_size("expert")
    gates = tasks * slots * exp_dev
    columns = np.arange(gates).reshape(tasks, slots, exp_dev).transpose(1, 2, 0).reshape(-1)
    order = np.zeros((gates, gates), np.float32)
    order[columns, np.arange(gates)] = 1.0
    outs = core(
        features, cross_weight[0], cross_bias, up_weight, down_weight,
        task_grad, gate_weight.T, gate_offset[None], jnp.asarray(order),
    )
    mixed, feature_grad, up_grad, down_grad, cross_grad, bias_grad, gating_grad, offset = outs
    return (
        mixed,
        feature_grad,
        up_grad,
        down_grad,
        cross_grad[None].astype(F32),
        bias_grad,
        gating_grad.T,
        offset.reshape(-1),
    )


def solution(mesh):
    placed = (
        P("dp", None),
        P(),
        P(),
        P(),
        P(),
        P("expert", None, "dp"),
        P("expert", "dp", None),
        P("dp", None, None),
    )
    return jax.shard_map(
        local,
        mesh=mesh,
        in_specs=placed,
        out_specs=(
            P("dp", None, None),
            P("dp", None),
            P("expert", None, "dp"),
            P("expert", "dp", None),
            P(),
            P(),
            P(),
            P(),
        ),
        check_vma=False,
    )
```
